128 devices in a mesh: seq: 32 (over z, x, core), ch: 4 (over y).
Axes of the slice: x: 4, y: 4, z: 4, core: 2. Of those that a mesh axis runs over, the one named last changes fastest.
Arguments:
- inputs: float32 [8192, 4096], P('seq', 'ch'), may hold values from -6 to 6
- out_grads: float32 [8192, 4096], P('seq', 'ch'), may hold values from -0.12 to 0.12
- tile_order: int32 [32], replicated, may hold values from 0 to 31, each once
- lag_order: int32 [32], replicated, may hold values from 0 to 31, each once
Outputs:
- filter_grad: float32 [256, 8192], P('ch', 'seq')
The draws below stay inside these ranges and needn't reach their ends.
Inputs may be any that keep to these rules, and one draw needn't show every extreme that they name: Row block i of inputs and out_grads holds sequence tile tile_order[i]; every tile appears once. Column block i of filter_grad holds lag block lag_order[i]; every lag block appears once.
All inputs are finite; a program needn't handle non-finite values.
Results may differ from the reference program's by a relative error of at most 0.000098.
Values sent between devices are 32-bit elements; how exact they have to be, the bound alone decides.
A program may use at most 128 MiB of HBM per device.

```python
import jax
import jax.numpy as jnp

TOK_DEV = 256
C = 4096
GROUP = 16
TOKENS = 8192
N_SEQ = 32


def steps_of(rng, extent, cuts, low, top_value):
    level, own = 1.0, jax.random.fold_in(rng, 6)
    for dim, blocks in cuts:
        heights = jnp.exp(jax.random.uniform(jax.random.fold_in(own, dim), (blocks,), jnp.float32, low / len(cuts), top_value / len(cuts)))
        level = level * jnp.repeat(heights, extent[dim] // blocks).reshape([-1 if axis == dim else 1 for axis in range(len(extent))])
    return level


def normal_values(rng, extent, scale, reach, pieces=(), kind=jnp.bfloat16):
    drawn = jax.random.normal(rng, extent, jnp.float32) * scale
    if len(pieces) > 0:
        drawn = steps_of(rng, extent, pieces, -0.22, 0.18) * drawn
    return jnp.clip(drawn, min=-reach, max=reach).astype(kind)


def setup_inputs(seed: int = 0) -> dict:
    streams_of = jax.random.split(jax.random.key(seed), 5)
    return {
        "inputs": normal_values(streams_of[0], (TOKENS, C), 1.0, 6.0, ((0, 32), (1, 4)), jnp.float32),
        "out_grads": normal_values(streams_of[1], (TOKENS, C), 0.02, 0.12, ((0, 32), (1, 4)), jnp.float32),
        "tile_order": jax.random.permutation(streams_of[2], N_SEQ).astype(jnp.int32),
        "lag_order": jax.random.permutation(streams_of[3], N_SEQ).astype(jnp.int32),
    }


target_ratio = 0.5
epsilon = 1e-12

def reference(inputs, out_grads, tile_order, lag_order):
    blocks = N_SEQ
    channels = inputs.shape[1]
    length = blocks * TOK_DEV
    natural_inputs = jnp.zeros((blocks, TOK_DEV, channels), jnp.float32).at[tile_order].set(inputs.reshape(blocks, TOK_DEV, channels)).reshape(length, channels)
    natural_grads = jnp.zeros((blocks, TOK_DEV, channels), jnp.float32).at[tile_order].set(out_grads.reshape(blocks, TOK_DEV, channels)).reshape(length, channels)
    input_spectrum = jnp.fft.rfft(natural_inputs, n=2 * length, axis=0)
    grad_spectrum = jnp.fft.rfft(natural_grads, n=2 * length, axis=0)
    correlation = jnp.fft.irfft(jnp.conj(input_spectrum) * grad_spectrum, n=2 * length, axis=0)[:length]
    grouped = correlation.reshape(length, channels // GROUP, GROUP).sum(axis=2).T
    squares = jnp.sum(grouped * grouped)
    factor = target_ratio * grouped.size ** 0.5 / jnp.sqrt(squares + epsilon)
    scaled = grouped * factor
    owned_blocks = scaled.reshape(channels // GROUP, blocks, TOK_DEV)[:, lag_order].reshape(channels // GROUP, length)
    return owned_blocks
```

```python
import functools
import math

import jax
import jax.numpy as jnp
import numpy as np
from jax import lax
from jax.experimental import pallas as pl
from jax.experimental.pallas import tpu as pltpu
from jax.sharding import PartitionSpec as P

C = 4096
GROUP = 16
target_ratio = 0.5
epsilon = 1e-12

MESH = pl.DeviceIdType.MESH
F32, BF16 = jnp.float32, jnp.bfloat16
SIDE = 4
POS = 16384
ROWS = 64
HOPS = (2, 1, 3, 0)
MOVES = tuple((d, k) for d in HOPS for k in (0, 1) if (d, k) != (0, 0))


def split(values):
    high = values.astype(BF16)
    return high, (values - high.astype(F32)).astype(BF16)


def dot3(left, right_high, right_low):
    high, low = split(left)
    dot = functools.partial(jnp.dot, preferred_element_type=F32)
    return dot(high, right_high) + (dot(low, right_high) + dot(high, right_low))


def tables():
    def halves(values):
        high = np.asarray(values, np.float32).astype(jnp.bfloat16)
        return high, (np.asarray(values, np.float32) - high.astype(np.float32)).astype(jnp.bfloat16)

    r = np.arange(128)
    angle = 2 * np.pi * (np.outer(r, r) % 128) / 128
    cos, sin = np.cos(angle), np.sin(angle)
    forward = np.block([[cos, -sin], [sin, cos]])
    inverse = np.block([[cos, sin], [-sin, cos]])
    m, n = np.divmod(np.arange(ROWS), 8)
    odd = 2 * (16 * n + m) + 1
    turn = np.pi * np.outer(odd, r) / POS
    twist = np.concatenate([np.cos(turn), np.sin(turn)], axis=1).astype(np.float32)
    step = 2 * np.arange(32)[None, :] + np.arange(2)[:, None]
    outer = np.pi * (np.outer(step.reshape(-1), odd) % 256) / 128
    ends = np.concatenate([np.cos(outer), -np.sin(outer)], axis=1) / (POS // 2)
    return halves(forward), halves(inverse), twist, halves(ends)


def place():
    me = lax.axis_index("seq")
    return me // 8, (me // 2) % 4, me % 2


def cmul(a, b, wr, wi):
    return a * wr - b * wi, a * wi + b * wr


def first_step(x):
    root = math.sqrt(0.5)
    s = [x[p + 4] * root for p in range(4)]
    plus = [x[p] + s[p] for p in range(4)]
    minus = [x[p] - s[p] for p in range(4)]
    out = [None] * 8
    for m in range(4):
        v = []
        for p in range(4):
            re = plus[p] if m in (0, 3) else minus[p]
            im = s[p]
            sign = -1.0 if m in (0, 1) else 1.0
            if p == 0:
                v.append((re, im if sign > 0 else -im))
            else:
                a = math.pi * (2 * m + 1) * p / 16
                wr, wi = math.cos(a), -math.sin(a)
                v.append((re * wr - im * (sign * wi), re * wi + im * (sign * wr)))
        e = (v[0][0] + v[2][0], v[0][1] + v[2][1])
        d = (v[0][0] - v[2][0], v[0][1] - v[2][1])
        f = (v[1][0] + v[3][0], v[1][1] + v[3][1])
        h = (v[1][0] - v[3][0], v[1][1] - v[3][1])
        out[m] = (e[0] + f[0], e[1] + f[1])
        out[m + 4] = (d[0] + h[1], d[1] - h[0])
    return out


def eight(z):
    add = lambda a, b: (a[0] + b[0], a[1] + b[1])
    sub = lambda a, b: (a[0] - b[0], a[1] - b[1])
    turn = lambda a: (a[1], -a[0])

    def four(a, b, c, d):
        e, f, g, h = add(a, c), sub(a, c), add(b, d), turn(sub(b, d))
        return add(e, g), add(f, h), sub(e, g), sub(f, h)

    even, odd = four(z[0], z[2], z[4], z[6]), four(z[1], z[3], z[5], z[7])
    root = math.sqrt(0.5)
    o1 = ((odd[1][0] + odd[1][1]) * root, (odd[1][1] - odd[1][0]) * root)
    o3 = ((odd[3][1] - odd[3][0]) * root, -(odd[3][0] + odd[3][1]) * root)
    turned = (odd[0], o1, turn(odd[2]), o3)
    return [add(even[k], turned[k]) for k in range(4)] + [sub(even[k], turned[k]) for k in range(4)]


def outer_steps(load, twist_ref, mid_ref, y_ref):
    def first(q2, carry):
        for half in range(2):
            out = first_step([load(4 * p + q2, half) for p in range(8)])
            for m in range(8):
                mid_ref[m, 2 * q2 + half, 0] = out[m][0]
                mid_ref[m, 2 * q2 + half, 1] = out[m][1]
        return carry

    lax.fori_loop(0, 4, first, 0)
    for m in range(8):
        z = []
        for q in range(8):
            re, im = mid_ref[m, q, 0], mid_ref[m, q, 1]
            a = math.pi * (2 * m + 1) * q / 128
            z.append((re, im) if q == 0 else cmul(re, im, math.cos(a), -math.sin(a)))
        for n, (re, im) in enumerate(eight(z)):
            row = 8 * m + n
            wr = twist_ref[pl.ds(row, 1), 0:128]
            wi = twist_ref[pl.ds(row, 1), 128:256]
            a, b = cmul(re, im, wr, -wi)
            y_ref[row, :, 0:128] = a
            y_ref[row, :, 128:256] = b


def transform(load, twist_ref, fh_ref, fl_ref, mid_ref, y_ref, spec_ref):
    outer_steps(load, twist_ref, mid_ref, y_ref)

    def rows(t, carry):
        at = pl.ds(t * 32, 32)
        spec_ref[at] = dot3(y_ref[at].reshape(256, 256), fh_ref[...], fl_ref[...]).reshape(32, 8, 256)
        return carry

    lax.fori_loop(0, ROWS // 32, rows, 0)


def multiply(u_ref, g_ref, acc_ref, fresh):
    def rows(t, carry):
        at = pl.ds(t * 4, 4)
        ur, ui = u_ref[at, :, 0:128], u_ref[at, :, 128:256]
        gr, gi = g_ref[at, :, 0:128], g_ref[at, :, 128:256]
        re, im = gr * ur + gi * ui, gi * ur - gr * ui
        if not fresh:
            re, im = re + acc_ref[at, :, 0:128], im + acc_ref[at, :, 128:256]
        acc_ref[at, :, 0:128] = re
        acc_ref[at, :, 128:256] = im
        return carry

    lax.fori_loop(0, ROWS // 4, rows, 0)


def to_lags(acc_ref, ih_ref, il_ref, twist_ref, eh_ref, el_ref):
    sums = jnp.sum(acc_ref[...], axis=1)
    v = dot3(sums, ih_ref[...], il_ref[...])
    re, im = cmul(v[:, 0:128], v[:, 128:256], twist_ref[:, 0:128], twist_ref[:, 128:256])
    high, low = split(jnp.concatenate([re, im], axis=0))
    dot = functools.partial(jnp.dot, preferred_element_type=F32)
    return dot(eh_ref[...], high) + (dot(eh_ref[...], low) + dot(el_ref[...], high))


def exchange_kernel(u_ref, g_ref, land, xin, turned, mid, insem, s_a, r_a, s_b, r_b, l_a, l_b):
    z, x, c = place()
    ch = lax.axis_index("ch")

    def device(kind, a, b, core):
        zz, xx = (b, a) if kind == 0 else (a, b)
        return (zz * 8 + xx * 2 + core, ch)

    mine = ((x, z), (z, x))
    incoming = []
    for step in HOPS:
        for kind in range(2):
            a = (mine[kind][0] + step) % SIDE
            for arr, ref in enumerate((u_ref, g_ref)):
                n = len(incoming)
                copy = pltpu.make_async_copy(
                    ref.at[:, pl.ds(pl.multiple_of(kind * 512 + a * 128, 128), 128)], xin.at[n], insem.at[n]
                )
                copy.start()
                incoming.append((copy, step, kind, a, arr))

    barrier = pltpu.get_barrier_semaphore()
    peers = [(kind, d, k) for kind in range(2) for d, k in MOVES if not (kind == 1 and d == 0)]
    for kind, d, k in peers:
        a, b = mine[kind]
        pl.semaphore_signal(barrier, inc=1, device_id=device(kind, (a + d) % SIDE, b, (c + k) % 2), device_id_type=MESH)
    pl.semaphore_wait(barrier, len(peers))

    def send_a(kind, kh, move):
        d, k = MOVES[move]
        a, b = mine[kind]
        to_a, to_c = (a + d) % SIDE, (c + k) % 2
        return pltpu.make_async_remote_copy(
            src_ref=turned.at[kind, to_a, to_c, :, kh],
            dst_ref=mid.at[kind, kh, :, a * 2 + c],
            send_sem=s_a.at[kind, kh, move],
            recv_sem=r_a.at[kind, kh, move],
            device_id=device(kind, to_a, b, to_c),
            device_id_type=MESH,
        )

    def own_a(kind, kh):
        a, _ = mine[kind]
        return pltpu.make_async_copy(turned.at[kind, a, c, :, kh], mid.at[kind, kh, :, a * 2 + c], l_a.at[kind, kh])

    def send_b(kind, kh, hop):
        a, b = mine[kind]
        to_b = (b + HOPS[hop]) % SIDE
        return pltpu.make_async_remote_copy(
            src_ref=mid.at[kind, kh, to_b],
            dst_ref=land.at[kind, kh, b],
            send_sem=s_b.at[kind, kh, hop],
            recv_sem=r_b.at[kind, kh, hop],
            device_id=device(kind, a, to_b, c),
            device_id_type=MESH,
        )

    def own_b(kind, kh):
        _, b = mine[kind]
        return pltpu.make_async_copy(mid.at[kind, kh, b], land.at[kind, kh, b], l_b.at[kind, kh])

    for n, (copy, step, kind, a, arr) in enumerate(incoming):
        copy.wait()
        turned[kind, a, :, :, :, arr] = xin[n].T.reshape(2, 4, 2, 8, 256)
        if arr == 1:
            for move, (d, k) in enumerate(MOVES):
                if d == step:
                    send_a(kind, 0, move).start()
            if step == 0:
                own_a(kind, 0).start()
    for kind in range(2):
        for move in range(len(MOVES)):
            send_a(kind, 1, move).start()
        own_a(kind, 1).start()
    for kh in range(2):
        for kind in range(2):
            own_a(kind, kh).wait()
            for move in range(len(MOVES)):
                send_a(kind, kh, move).wait_recv()
            for hop in range(3):
                send_b(kind, kh, hop).start()
            own_b(kind, kh).start()
    for kh in range(2):
        for kind in range(2):
            own_b(kind, kh).wait()
            for hop in range(3):
                send_b(kind, kh, hop).wait()
            for move in range(len(MOVES)):
                send_a(kind, kh, move).wait_send()


def compute_kernel(tiles, lags, land, fh, fl, ih, il, twist, eh, el, blocks, slots, mid_ref, y_ref, su_ref, sg_ref, acc_ref, lag_ref):
    def invert(s, carry):
        zz, xx, cc = s // 8, (s // 2) % 4, s % 2
        tile = tiles[s]
        slots[0, tile] = s
        slots[1, tile] = xx * 8 + zz * 2 + cc
        return carry

    lax.fori_loop(0, 32, invert, 0)
    squares = jnp.zeros((1, 128), F32)
    for kind in range(2):
        for kh in range(2):
            for arr, spec in enumerate((su_ref, sg_ref)):
                load = lambda tile, half: land[kind, kh, slots[kind, tile], arr, :, half * 128 : half * 128 + 128]
                transform(load, twist, fh, fl, mid_ref, y_ref, spec)
            multiply(su_ref, sg_ref, acc_ref, kh == 0)
        values = to_lags(acc_ref, ih, il, twist, eh, el)
        lag_ref[kind] = values
        squares = squares + jnp.sum(values * values, axis=0, keepdims=True)

    def pack(s, carry):
        zz, xx, cc = s // 8, (s // 2) % 4, s % 2
        block = lags[s]
        for kind in range(2):
            for half in range(2):
                blocks[xx, cc, zz, pl.ds(2 * kind + half, 1), :] = lag_ref[kind, pl.ds(half * 32 + block, 1), :]
        blocks[xx, cc, zz, pl.ds(4, 1), :] = squares
        return carry

    lax.fori_loop(0, 32, pack, 0)


def owners_kernel(blocks, out, total, mid, land, tally, sums, s_a, r_a, s_b, r_b, s_q, r_q, l_a, l_b):
    z, x, c = place()
    ch = lax.axis_index("ch")
    barrier = pltpu.get_barrier_semaphore()
    moves = MOVES
    far = [(dz, dy) for dz in HOPS for dy in HOPS if (dz, dy) != (0, 0)]

    def at(zz, xx, cc, yy):
        return (zz * 8 + xx * 2 + cc, yy)

    peers = [at(z, (x + d) % SIDE, (c + k) % 2, ch) for d, k in moves]
    peers += [at((z + dz) % SIDE, x, c, (ch + dy) % SIDE) for dz, dy in far]
    for peer in peers:
        pl.semaphore_signal(barrier, inc=1, device_id=peer, device_id_type=MESH)
    pl.semaphore_wait(barrier, len(peers))

    def send_a(move):
        d, k = moves[move]
        to_x, to_c = (x + d) % SIDE, (c + k) % 2
        return pltpu.make_async_remote_copy(
            src_ref=blocks.at[to_x, to_c],
            dst_ref=mid.at[:, x * 2 + c],
            send_sem=s_a.at[move],
            recv_sem=r_a.at[move],
            device_id=at(z, to_x, to_c, ch),
            device_id_type=MESH,
        )

    def send_b(hop):
        to_z = (z + HOPS[hop]) % SIDE
        return pltpu.make_async_remote_copy(
            src_ref=mid.at[to_z],
            dst_ref=land.at[z],
            send_sem=s_b.at[hop],
            recv_sem=r_b.at[hop],
            device_id=at(to_z, x, c, ch),
            device_id_type=MESH,
        )

    def send_q(k):
        dz, dy = far[k]
        return pltpu.make_async_remote_copy(
            src_ref=sums,
            dst_ref=tally.at[k],
            send_sem=s_q.at[k],
            recv_sem=r_q.at[k],
            device_id=at((z + dz) % SIDE, x, c, (ch + dy) % SIDE),
            device_id_type=MESH,
        )

    own_a = pltpu.make_async_copy(blocks.at[x, c], mid.at[:, x * 2 + c], l_a)
    own_a.start()
    for move in range(len(moves)):
        send_a(move).start()
    own_a.wait()
    for move in range(len(moves)):
        send_a(move).wait_recv()
    own_b = pltpu.make_async_copy(mid.at[z], land.at[z], l_b)
    own_b.start()
    for hop in range(3):
        send_b(hop).start()
    sums[...] = jnp.sum(mid[0], axis=0)
    for k in range(len(far)):
        send_q(k).start()
    own_b.wait()
    for hop in range(3):
        send_b(hop).wait_recv()

    for s in range(32):
        zz, xc = s // 8, s % 8
        xx, cc = xc // 2, xc % 2
        for kind in range(2):
            row = (2 * xx + cc) * 4 + zz if kind == 0 else 32 + (2 * zz + cc) * 4 + xx
            for half in range(2):
                out[row : row + 1, half * 128 : half * 128 + 128] = land[zz, xc, 2 * kind + half : 2 * kind + half + 1, :]
    for k in range(len(far)):
        send_q(k).wait_recv()
    total[...] = (sums[...] + jnp.sum(tally[...], axis=0))[4:5]
    for move in range(len(moves)):
        send_a(move).wait_send()
    for hop in range(3):
        send_b(hop).wait_send()
    for k in range(len(far)):
        send_q(k).wait_send()


def shards(inputs, out_grads, tile_order, lag_order):
    vmem = pl.BlockSpec(memory_space=pltpu.VMEM)
    smem = pl.BlockSpec(memory_space=pltpu.SMEM)
    hbm = pl.BlockSpec(memory_space=pl.ANY)
    dma = pltpu.SemaphoreType.DMA
    sds = jax.ShapeDtypeStruct
    land = pl.pallas_call(
        exchange_kernel,
        out_shape=sds((2, 2, 4, 8, 2, 8, 256), F32),
        in_specs=[hbm, hbm],
        out_specs=vmem,
        scratch_shapes=[
            pltpu.VMEM((16, 256, 128), F32),
            pltpu.VMEM((2, 4, 2, 4, 2, 2, 8, 256), F32),
            pltpu.VMEM((2, 2, 4, 8, 2, 8, 256), F32),
            dma((16,)), dma((2, 2, 7)), dma((2, 2, 7)), dma((2, 2, 3)), dma((2, 2, 3)), dma((2, 2)), dma((2, 2)),
        ],
        compiler_params=pltpu.CompilerParams(collective_id=0, has_side_effects=True),
    )(inputs, out_grads)
    (fh, fl), (ih, il), twist, (eh, el) = tables()
    consts = [jnp.asarray(t) for t in (fh, fl, ih, il, twist, eh, el)]
    blocks = pl.pallas_call(
        compute_kernel,
        out_shape=sds((4, 2, 4, 8, 128), F32),
        in_specs=[smem, smem, vmem] + [vmem] * 7,
        out_specs=vmem,
        scratch_shapes=[
            pltpu.SMEM((2, 32), jnp.int32),
            pltpu.VMEM((8, 8, 2, 8, 128), F32),
            pltpu.VMEM((ROWS, 8, 256), F32),
            pltpu.VMEM((ROWS, 8, 256), F32),
            pltpu.VMEM((ROWS, 8, 256), F32),
            pltpu.VMEM((ROWS, 8, 256), F32),
            pltpu.VMEM((2, ROWS, 128), F32),
        ],
    )(tile_order, lag_order, land.reshape(2, 2, 32, 2, 8, 256), *consts)
    owned, total = pl.pallas_call(
        owners_kernel,
        out_shape=(sds((64, 256), F32), sds((1, 128), F32)),
        in_specs=[vmem],
        out_specs=(vmem, vmem),
        scratch_shapes=[
            pltpu.VMEM((4, 8, 8, 128), F32),
            pltpu.VMEM((4, 8, 8, 128), F32),
            pltpu.VMEM((15, 8, 128), F32),
            pltpu.VMEM((8, 128), F32),
            dma((7,)), dma((7,)), dma((3,)), dma((3,)), dma((15,)), dma((15,)), dma, dma,
        ],
        compiler_params=pltpu.CompilerParams(collective_id=1, has_side_effects=True),
    )(blocks)
    squares = jnp.sum(total)
    total_entries = C // GROUP * POS // 2
    factor = target_ratio * math.sqrt(total_entries) / jnp.sqrt(squares + epsilon)
    return owned * factor


def solution(mesh):
    return jax.shard_map(
        shards,
        mesh=mesh,
        in_specs=(P("seq", "ch"), P("seq", "ch"), P(), P()),
        out_specs=P("ch", "seq"),
        check_vma=False,
    )
```

```python
import functools
import math

import jax
import jax.numpy as jnp
import numpy as np
from jax import lax
from jax.experimental import pallas as pl
from jax.experimental.pallas import tpu as pltpu
from jax.sharding import PartitionSpec as P

C = 4096
GROUP = 16
target_ratio = 0.5
epsilon = 1e-12

MESH = pl.DeviceIdType.MESH
F32, BF16 = jnp.float32, jnp.bfloat16
SIDE = 4
POS = 16384
ROWS = 64
HOPS = (2, 1, 3, 0)
MOVES = tuple((d, k) for d in HOPS for k in (0, 1) if (d, k) != (0, 0))


def split(values):
    high = values.astype(BF16)
    return high, (values - high.astype(F32)).astype(BF16)


def dot3(left, right_high, right_low):
    high, low = split(left)
    dot = functools.partial(jnp.dot, preferred_element_type=F32)
    return dot(high, right_high) + (dot(low, right_high) + dot(high, right_low))


def tables():
    def halves(values):
        high = np.asarray(values, np.float32).astype(jnp.bfloat16)
        return high, (np.asarray(values, np.float32) - high.astype(np.float32)).astype(jnp.bfloat16)

    r = np.arange(128)
    angle = 2 * np.pi * (np.outer(r, r) % 128) / 128
    cos, sin = np.cos(angle), np.sin(angle)
    forward = np.block([[cos, -sin], [sin, cos]])
    inverse = np.block([[cos, sin], [-sin, cos]])
    m, n = np.divmod(np.arange(ROWS), 8)
    odd = 2 * (16 * n + m) + 1
    turn = np.pi * np.outer(odd, r) / POS
    twist = np.concatenate([np.cos(turn), np.sin(turn)], axis=1).astype(np.float32)
    step = 2 * np.arange(32)[None, :] + np.arange(2)[:, None]
    outer = np.pi * (np.outer(step.reshape(-1), odd) % 256) / 128
    ends = np.concatenate([np.cos(outer), -np.sin(outer)], axis=1) / (POS // 2)
    return halves(forward), halves(inverse), twist, halves(ends)


def place():
    me = lax.axis_index("seq")
    return me // 8, (me // 2) % 4, me % 2


def cmul(a, b, wr, wi):
    return a * wr - b * wi, a * wi + b * wr


def first_step(x):
    root = math.sqrt(0.5)
    s = [x[p + 4] * root for p in range(4)]
    plus = [x[p] + s[p] for p in range(4)]
    minus = [x[p] - s[p] for p in range(4)]
    out = [None] * 8
    for m in range(4):
        v = []
        for p in range(4):
            re = plus[p] if m in (0, 3) else minus[p]
            im = s[p]
            sign = -1.0 if m in (0, 1) else 1.0
            if p == 0:
                v.append((re, im if sign > 0 else -im))
            else:
                a = math.pi * (2 * m + 1) * p / 16
                wr, wi = math.cos(a), -math.sin(a)
                v.append((re * wr - im * (sign * wi), re * wi + im * (sign * wr)))
        e = (v[0][0] + v[2][0], v[0][1] + v[2][1])
        d = (v[0][0] - v[2][0], v[0][1] - v[2][1])
        f = (v[1][0] + v[3][0], v[1][1] + v[3][1])
        h = (v[1][0] - v[3][0], v[1][1] - v[3][1])
        out[m] = (e[0] + f[0], e[1] + f[1])
        out[m + 4] = (d[0] + h[1], d[1] - h[0])
    return out


def eight(z):
    add = lambda a, b: (a[0] + b[0], a[1] + b[1])
    sub = lambda a, b: (a[0] - b[0], a[1] - b[1])
    turn = lambda a: (a[1], -a[0])

    def four(a, b, c, d):
        e, f, g, h = add(a, c), sub(a, c), add(b, d), turn(sub(b, d))
        return add(e, g), add(f, h), sub(e, g), sub(f, h)

    even, odd = four(z[0], z[2], z[4], z[6]), four(z[1], z[3], z[5], z[7])
    root = math.sqrt(0.5)
    o1 = ((odd[1][0] + odd[1][1]) * root, (odd[1][1] - odd[1][0]) * root)
    o3 = ((odd[3][1] - odd[3][0]) * root, -(odd[3][0] + odd[3][1]) * root)
    turned = (odd[0], o1, turn(odd[2]), o3)
    return [add(even[k], turned[k]) for k in range(4)] + [sub(even[k], turned[k]) for k in range(4)]


def outer_steps(load, twist_ref, mid_ref, y_ref):
    def first(q2, carry):
        for half in range(2):
            out = first_step([load(4 * p + q2, half) for p in range(8)])
            for m in range(8):
                mid_ref[m, 2 * q2 + half, 0] = out[m][0]
                mid_ref[m, 2 * q2 + half, 1] = out[m][1]
        return carry

    lax.fori_loop(0, 4, first, 0)
    for m in range(8):
        z = []
        for q in range(8):
            re, im = mid_ref[m, q, 0], mid_ref[m, q, 1]
            a = math.pi * (2 * m + 1) * q / 128
            z.append((re, im) if q == 0 else cmul(re, im, math.cos(a), -math.sin(a)))
        for n, (re, im) in enumerate(eight(z)):
            row = 8 * m + n
            wr = twist_ref[pl.ds(row, 1), 0:128]
            wi = twist_ref[pl.ds(row, 1), 128:256]
            a, b = cmul(re, im, wr, -wi)
            y_ref[row, :, 0:128] = a
            y_ref[row, :, 128:256] = b


def transform(load, twist_ref, fh_ref, fl_ref, mid_ref, y_ref, spec_ref):
    outer_steps(load, twist_ref, mid_ref, y_ref)

    def rows(t, carry):
        at = pl.ds(t * 32, 32)
        spec_ref[at] = dot3(y_ref[at].reshape(256, 256), fh_ref[...], fl_ref[...]).reshape(32, 8, 256)
        return carry

    lax.fori_loop(0, ROWS // 32, rows, 0)


def multiply(u_ref, g_ref, acc_ref, fresh):
    def rows(t, carry):
        at = pl.ds(t * 4, 4)
        ur, ui = u_ref[at, :, 0:128], u_ref[at, :, 128:256]
        gr, gi = g_ref[at, :, 0:128], g_ref[at, :, 128:256]
        re, im = gr * ur + gi * ui, gi * ur - gr * ui
        if not fresh:
            re, im = re + acc_ref[at, :, 0:128], im + acc_ref[at, :, 128:256]
        acc_ref[at, :, 0:128] = re
        acc_ref[at, :, 128:256] = im
        return carry

    lax.fori_loop(0, ROWS // 4, rows, 0)


def to_lags(acc_ref, ih_ref, il_ref, twist_ref, eh_ref, el_ref):
    sums = jnp.sum(acc_ref[...], axis=1)
    v = dot3(sums, ih_ref[...], il_ref[...])
    re, im = cmul(v[:, 0:128], v[:, 128:256], twist_ref[:, 0:128], twist_ref[:, 128:256])
    high, low = split(jnp.concatenate([re, im], axis=0))
    dot = functools.partial(jnp.dot, preferred_element_type=F32)
    return dot(eh_ref[...], high) + (dot(eh_ref[...], low) + dot(el_ref[...], high))


def fused_kernel(tiles, lags, u_ref, g_ref, *refs):
    tables_hbm, refs = refs[:7], refs[7:]
    out, refs = refs[0], refs[1:]
    tables_vmem, refs = refs[:7], refs[7:]
    fh, fl, ih, il, twist, eh, el = tables_vmem
    (slots, xin, turned, mid, land, stage, mid_ref, y_ref, su_ref, sg_ref, acc_ref, lag_ref, blocks, mid_o, land_o, tally, sums,
     insem, tabsem, s_a, r_a, s_b, r_b, l_a, l_b, s_ao, r_ao, s_bo, r_bo, s_q, r_q, l_o) = refs
    z, x, c = place()
    ch = lax.axis_index("ch")

    def at(dz, dx, dc, dy):
        return (((z + dz) % SIDE) * 8 + ((x + dx) % SIDE) * 2 + (c + dc) % 2, (ch + dy) % SIDE)

    def shift(kind, d, k, e):
        return at(e, d, k, 0) if kind == 0 else at(d, e, k, 0)

    mine = ((x, z), (z, x))
    incoming = []
    for arr, ref in enumerate((u_ref, g_ref)):
        for step in HOPS:
            for kind in range(2):
                a = (mine[kind][0] + step) % SIDE
                n = len(incoming)
                copy = pltpu.make_async_copy(
                    ref.at[:, pl.ds(pl.multiple_of(kind * 512 + a * 128, 128), 128)], xin.at[n], insem.at[n]
                )
                copy.start()
                incoming.append((copy, step, kind, a, arr))
    table_copies = [pltpu.make_async_copy(h, v, tabsem.at[n]) for n, (h, v) in enumerate(zip(tables_hbm, tables_vmem))]
    for copy in table_copies:
        copy.start()

    far = [(dz, dy) for dz in HOPS for dy in HOPS if (dz, dy) != (0, 0)]
    peers = {(0, d, k, 0) for d, k in MOVES} | {(d, 0, k, 0) for d, k in MOVES} | {(dz, 0, 0, dy) for dz, dy in far}
    peers = sorted(peers)
    barrier = pltpu.get_barrier_semaphore()
    for peer in peers:
        pl.semaphore_signal(barrier, inc=1, device_id=at(*peer), device_id_type=MESH)
    pl.semaphore_wait(barrier, len(peers))

    def send_a(kind, kh, arr, move):
        d, k = MOVES[move]
        a = mine[kind][0]
        return pltpu.make_async_remote_copy(
            src_ref=turned.at[kind, (a + d) % SIDE, (c + k) % 2, :, kh, arr],
            dst_ref=mid.at[kind, kh, arr, :, a * 2 + c],
            send_sem=s_a.at[kind, kh, arr, move],
            recv_sem=r_a.at[kind, kh, arr, move],
            device_id=shift(kind, d, k, 0),
            device_id_type=MESH,
        )

    def own_a(kind, kh, arr):
        a = mine[kind][0]
        return pltpu.make_async_copy(
            turned.at[kind, a, c, :, kh, arr], mid.at[kind, kh, arr, :, a * 2 + c], l_a.at[kind, kh, arr]
        )

    def send_b(kind, kh, arr, hop):
        b = mine[kind][1]
        return pltpu.make_async_remote_copy(
            src_ref=mid.at[kind, kh, arr, (b + HOPS[hop]) % SIDE],
            dst_ref=land.at[kind, kh, arr, pl.ds(b * 8, 8)],
            send_sem=s_b.at[kind, kh, arr, hop],
            recv_sem=r_b.at[kind, kh, arr, hop],
            device_id=shift(kind, 0, 0, HOPS[hop]),
            device_id_type=MESH,
        )

    def own_b(kind, kh, arr):
        b = mine[kind][1]
        return pltpu.make_async_copy(
            mid.at[kind, kh, arr, b], land.at[kind, kh, arr, pl.ds(b * 8, 8)], l_b.at[kind, kh, arr]
        )

    for n, (copy, step, kind, a, arr) in enumerate(incoming):
        copy.wait()
        turned[kind, a, :, :, :, arr] = xin[n].T.reshape(2, 4, 2, 8, 256)
        for move, (d, k) in enumerate(MOVES):
            if d == step:
                send_a(kind, 0, arr, move).start()
        if step == 0:
            own_a(kind, 0, arr).start()
    for arr in range(2):
        for move in range(len(MOVES)):
            for kind in range(2):
                send_a(kind, 1, arr, move).start()
        for kind in range(2):
            own_a(kind, 1, arr).start()

    def find(tile, carry):
        first, second = jnp.int32(0), jnp.int32(0)
        for s in range(32):
            zz, xx, cc = s // 8, (s // 2) % 4, s % 2
            hit = tiles[s] == tile
            first = jnp.where(hit, s, first)
            second = jnp.where(hit, xx * 8 + zz * 2 + cc, second)
        slots[0, tile] = first
        slots[1, tile] = second
        return carry

    lax.fori_loop(0, 32, find, 0)

    for kh in range(2):
        for arr in range(2):
            for kind in range(2):
                own_a(kind, kh, arr).wait()
                for move in range(len(MOVES)):
                    send_a(kind, kh, arr, move).wait_recv()
                for hop in range(3):
                    send_b(kind, kh, arr, hop).start()
                own_b(kind, kh, arr).start()
    for copy in table_copies:
        copy.wait()
    acc_ref[...] = jnp.zeros_like(acc_ref)

    def chunk(kh, carry):
        for arr, spec in enumerate((su_ref, sg_ref)):
            for kind in range(2):
                own_b(kind, kh, arr).wait()
                for hop in range(3):
                    send_b(kind, kh, arr, hop).wait_recv()
                stage[...] = land[kind, kh, arr]
                load = lambda tile, half: stage[slots[kind, tile], :, half * 128 : half * 128 + 128]
                transform(load, twist, fh, fl, mid_ref, y_ref, spec.at[kind])
                if arr == 1:
                    multiply(su_ref.at[kind], sg_ref.at[kind], acc_ref.at[kind], False)
        return carry

    lax.fori_loop(0, 2, chunk, 0)
    squares = jnp.zeros((1, 128), F32)
    for kind in range(2):
        values = to_lags(acc_ref.at[kind], ih, il, twist, eh, el)
        lag_ref[kind] = values
        squares = squares + jnp.sum(values * values, axis=0, keepdims=True)

    def send_ao(move):
        d, k = MOVES[move]
        return pltpu.make_async_remote_copy(
            src_ref=blocks.at[(x + d) % SIDE, (c + k) % 2],
            dst_ref=mid_o.at[:, x * 2 + c],
            send_sem=s_ao.at[move],
            recv_sem=r_ao.at[move],
            device_id=at(0, d, k, 0),
            device_id_type=MESH,
        )

    def send_bo(hop):
        return pltpu.make_async_remote_copy(
            src_ref=mid_o.at[(z + HOPS[hop]) % SIDE],
            dst_ref=land_o.at[z],
            send_sem=s_bo.at[hop],
            recv_sem=r_bo.at[hop],
            device_id=at(HOPS[hop], 0, 0, 0),
            device_id_type=MESH,
        )

    def send_q(k):
        return pltpu.make_async_remote_copy(
            src_ref=sums,
            dst_ref=tally.at[k],
            send_sem=s_q.at[k],
            recv_sem=r_q.at[k],
            device_id=at(far[k][0], 0, 0, far[k][1]),
            device_id_type=MESH,
        )

    def pack(s, carry):
        zz, xx, cc = s // 8, (s // 2) % 4, s % 2
        block = lags[s]
        for kind in range(2):
            for half in range(2):
                blocks[xx, cc, zz, pl.ds(2 * kind + half, 1), :] = lag_ref[kind, pl.ds(half * 32 + block, 1), :]
        blocks[xx, cc, zz, pl.ds(4, 1), :] = squares
        return carry

    lax.fori_loop(0, 32, pack, 0)
    own_ao = pltpu.make_async_copy(blocks.at[x, c], mid_o.at[:, x * 2 + c], l_o.at[0])
    own_ao.start()
    for move in range(len(MOVES)):
        send_ao(move).start()
    own_ao.wait()
    for move in range(len(MOVES)):
        send_ao(move).wait_recv()
    own_bo = pltpu.make_async_copy(mid_o.at[z], land_o.at[z], l_o.at[1])
    own_bo.start()
    for hop in range(3):
        send_bo(hop).start()
    sums[...] = jnp.sum(mid_o[0], axis=0)
    for k in range(len(far)):
        send_q(k).start()
    for kh in range(2):
        for arr in range(2):
            for kind in range(2):
                for move in range(len(MOVES)):
                    send_a(kind, kh, arr, move).wait_send()
                for hop in range(3):
                    send_b(kind, kh, arr, hop).wait_send()
    for move in range(len(MOVES)):
        send_ao(move).wait_send()
    for k in range(len(far)):
        send_q(k).wait_recv()
    total = jnp.sum((sums[...] + jnp.sum(tally[...], axis=0))[4:5], axis=1, keepdims=True)
    total_entries = C // GROUP * POS // 2
    factor = target_ratio * math.sqrt(total_entries) / jnp.sqrt(total + epsilon)
    own_bo.wait()
    for hop in range(3):
        send_bo(hop).wait_recv()
    for s in range(32):
        zz, xc = s // 8, s % 8
        xx, cc = xc // 2, xc % 2
        for kind in range(2):
            row = (2 * xx + cc) * 4 + zz if kind == 0 else 32 + (2 * zz + cc) * 4 + xx
            for half in range(2):
                values = land_o[zz, xc, 2 * kind + half : 2 * kind + half + 1, :]
                out[row : row + 1, half * 128 : half * 128 + 128] = values * factor
    for hop in range(3):
        send_bo(hop).wait_send()
    for k in range(len(far)):
        send_q(k).wait_send()


def shards(inputs, out_grads, tile_order, lag_order):
    vmem = pl.BlockSpec(memory_space=pltpu.VMEM)
    smem = pl.BlockSpec(memory_space=pltpu.SMEM)
    hbm = pl.BlockSpec(memory_space=pl.ANY)
    dma = pltpu.SemaphoreType.DMA
    (fh, fl), (ih, il), twist, (eh, el) = tables()
    consts = [jnp.asarray(t) for t in (fh, fl, ih, il, twist, eh, el)]
    return pl.pallas_call(
        fused_kernel,
        out_shape=jax.ShapeDtypeStruct((64, 256), F32),
        in_specs=[smem, smem] + [hbm] * 9,
        out_specs=vmem,
        scratch_shapes=[pltpu.VMEM(t.shape, t.dtype) for t in consts]
        + [
            pltpu.SMEM((2, 32), jnp.int32),
            pltpu.VMEM((16, 256, 128), F32),
            pltpu.VMEM((2, 4, 2, 4, 2, 2, 8, 256), F32),
            pltpu.VMEM((2, 2, 2, 4, 8, 8, 256), F32),
            pltpu.VMEM((2, 2, 2, 32, 8, 256), F32),
            pltpu.VMEM((32, 8, 256), F32),
            pltpu.VMEM((8, 8, 2, 8, 128), F32),
            pltpu.VMEM((ROWS, 8, 256), F32),
            pltpu.VMEM((2, ROWS, 8, 256), F32),
            pltpu.VMEM((2, ROWS, 8, 256), F32),
            pltpu.VMEM((2, ROWS, 8, 256), F32),
            pltpu.VMEM((2, ROWS, 128), F32),
            pltpu.VMEM((4, 2, 4, 8, 128), F32),
            pltpu.VMEM((4, 8, 8, 128), F32),
            pltpu.VMEM((4, 8, 8, 128), F32),
            pltpu.VMEM((15, 8, 128), F32),
            pltpu.VMEM((8, 128), F32),
            dma((16,)), dma((7,)), dma((2, 2, 2, 7)), dma((2, 2, 2, 7)), dma((2, 2, 2, 3)), dma((2, 2, 2, 3)),
            dma((2, 2, 2)), dma((2, 2, 2)), dma((7,)), dma((7,)), dma((3,)), dma((3,)), dma((15,)), dma((15,)), dma((2,)),
        ],
        compiler_params=pltpu.CompilerParams(collective_id=0, has_side_effects=True),
    )(tile_order, lag_order, inputs, out_grads, *consts)


def solution(mesh):
    return jax.shard_map(
        shards,
        mesh=mesh,
        in_specs=(P("seq", "ch"), P("seq", "ch"), P(), P()),
        out_specs=P("ch", "seq"),
        check_vma=False,
    )
```

```python
import functools
import math

import jax
import jax.numpy as jnp
import numpy as np
from jax import lax
from jax.experimental import pallas as pl
from jax.experimental.pallas import tpu as pltpu
from jax.sharding import PartitionSpec as P

C = 4096
GROUP = 16
target_ratio = 0.5
epsilon = 1e-12

MESH = pl.DeviceIdType.MESH
F32, BF16 = jnp.float32, jnp.bfloat16
SIDE = 4
POS = 16384
ROWS = 64
HOPS = (2, 1, 3, 0)
MOVES = tuple((d, k) for d in HOPS for k in (0, 1) if (d, k) != (0, 0))


def split(values):
    high = values.astype(BF16)
    return high, (values - high.astype(F32)).astype(BF16)


def dot3(left, right):
    dot = functools.partial(jnp.dot, preferred_element_type=F32)
    return dot(left[0], right[0]) + (dot(left[1], right[0]) + dot(left[0], right[1]))


def tables():
    def halves(values):
        high = np.asarray(values, np.float32).astype(jnp.bfloat16)
        return high, (np.asarray(values, np.float32) - high.astype(np.float32)).astype(jnp.bfloat16)

    r = np.arange(128)
    angle = 2 * np.pi * (np.outer(r, r) % 128) / 128
    cos, sin = np.cos(angle), np.sin(angle)
    forward = np.block([[cos, -sin], [sin, cos]])
    inverse = np.block([[cos, sin], [-sin, cos]])
    m, n = np.divmod(np.arange(ROWS), 8)
    odd = 2 * (16 * n + m) + 1
    turn = np.pi * np.outer(odd, r) / POS
    twist = np.concatenate([np.cos(turn), np.sin(turn)], axis=1).astype(np.float32)
    step = 2 * np.arange(32)[None, :] + np.arange(2)[:, None]
    outer = np.pi * (np.outer(step.reshape(-1), odd) % 256) / 128
    ends = np.concatenate([np.cos(outer), -np.sin(outer)], axis=1) / (POS // 2)
    return (*halves(forward), *halves(inverse), twist, ends.astype(np.float32))


def place():
    me = lax.axis_index("seq")
    return me // 8, (me // 2) % 4, me % 2


def cmul(a, b, wr, wi):
    return a * wr - b * wi, a * wi + b * wr


def first_step(x):
    root = math.sqrt(0.5)
    s = [x[p + 4] * root for p in range(4)]
    plus = [x[p] + s[p] for p in range(4)]
    minus = [x[p] - s[p] for p in range(4)]
    out = [None] * 8
    for m in range(4):
        v = []
        for p in range(4):
            re = plus[p] if m in (0, 3) else minus[p]
            im = s[p]
            sign = -1.0 if m in (0, 1) else 1.0
            if p == 0:
                v.append((re, im if sign > 0 else -im))
            else:
                a = math.pi * (2 * m + 1) * p / 16
                wr, wi = math.cos(a), -math.sin(a)
                v.append((re * wr - im * (sign * wi), re * wi + im * (sign * wr)))
        e = (v[0][0] + v[2][0], v[0][1] + v[2][1])
        d = (v[0][0] - v[2][0], v[0][1] - v[2][1])
        f = (v[1][0] + v[3][0], v[1][1] + v[3][1])
        h = (v[1][0] - v[3][0], v[1][1] - v[3][1])
        out[m] = (e[0] + f[0], e[1] + f[1])
        out[m + 4] = (d[0] + h[1], d[1] - h[0])
    return out


def eight(z):
    add = lambda a, b: (a[0] + b[0], a[1] + b[1])
    sub = lambda a, b: (a[0] - b[0], a[1] - b[1])
    turn = lambda a: (a[1], -a[0])

    def four(a, b, c, d):
        e, f, g, h = add(a, c), sub(a, c), add(b, d), turn(sub(b, d))
        return add(e, g), add(f, h), sub(e, g), sub(f, h)

    even, odd = four(z[0], z[2], z[4], z[6]), four(z[1], z[3], z[5], z[7])
    root = math.sqrt(0.5)
    o1 = ((odd[1][0] + odd[1][1]) * root, (odd[1][1] - odd[1][0]) * root)
    o3 = ((odd[3][1] - odd[3][0]) * root, -(odd[3][0] + odd[3][1]) * root)
    turned = (odd[0], o1, turn(odd[2]), o3)
    return [add(even[k], turned[k]) for k in range(4)] + [sub(even[k], turned[k]) for k in range(4)]


def outer_first(load, mid_ref):
    for q2 in range(4):
        for half in range(2):
            out = first_step([load(4 * p + q2, half) for p in range(8)])
            for m in range(8):
                mid_ref[m, 2 * q2 + half, 0] = out[m][0]
                mid_ref[m, 2 * q2 + half, 1] = out[m][1]


def outer_second(twist_ref, mid_ref, y_ref):
    for m in range(8):
        z = []
        for q in range(8):
            re, im = mid_ref[m, q, 0], mid_ref[m, q, 1]
            a = math.pi * (2 * m + 1) * q / 128
            z.append((re, im) if q == 0 else cmul(re, im, math.cos(a), -math.sin(a)))
        done = []
        for n, (re, im) in enumerate(eight(z)):
            row = 8 * m + n
            done.append(cmul(re, im, twist_ref[row : row + 1, 0:128], -twist_ref[row : row + 1, 128:256]))
        for n in range(0, 8, 2):
            for part in range(2):
                pair = split(jnp.concatenate([done[n][part], done[n + 1][part]], axis=0))
                for k in range(2):
                    y_ref[k, (8 * m + n) * 8 : (8 * m + n) * 8 + 16, part * 128 : part * 128 + 128] = pair[k]


def inner(y_ref, at, table):
    return dot3((y_ref[0, at : at + 256], y_ref[1, at : at + 256]), table)


def channel_sums(rows):
    lane = lax.broadcasted_iota(jnp.int32, (8, 128), 0)
    low = lane < 4
    out = []
    for k in range(4):
        a, b = rows[k], rows[k + 4]
        out.append(jnp.where(low, a, b) + pltpu.roll(jnp.where(low, b, a), 4, 0))
    for width in (2, 1):
        keep = lane % (2 * width) < width
        out = [
            jnp.where(keep, a + pltpu.roll(a, 8 - width, 0), b + pltpu.roll(b, width, 0))
            for a, b in zip(out[:width], out[width:])
        ]
    return out[0]


def multiply(grads, spec_ref, at, acc_ref):
    for m in range(4):
        re, im = [], []
        for n in range(8):
            row = m * 64 + n * 8
            gr, gi = grads[row : row + 8, 0:128], grads[row : row + 8, 128:256]
            ur, ui = spec_ref[at + row : at + row + 8, 0:128], spec_ref[at + row : at + row + 8, 128:256]
            re.append(gr * ur + gi * ui)
            im.append(gi * ur - gr * ui)
        to = at // 8 + m * 8
        acc_ref[to : to + 8, 0:128] += channel_sums(re)
        acc_ref[to : to + 8, 128:256] += channel_sums(im)


def fused_kernel(tiles, lags, u_ref, g_ref, *refs):
    tables_hbm, refs = refs[:6], refs[6:]
    out, refs = refs[0], refs[1:]
    tables_vmem, refs = refs[:6], refs[6:]
    fh, fl, ih, il, twist, ends = tables_vmem
    (slots, xin, turned, mid, land, stage, mid_ref, y_a, y_b, spec_ref, acc_ref, ends_f, ends_b, blocks, mid_o, land_o,
     owned, square, near_sq, sums, tally,
     insem, tabsem, s_a, r_a, s_b, r_b, l_a, l_b, s_ao, r_ao, s_bo, r_bo, s_n, r_n, s_q, r_q, l_o, far_sem) = refs
    z, x, c = place()
    ch = lax.axis_index("ch")

    def at(dz, dx, dc, dy):
        return (((z + dz) % SIDE) * 8 + ((x + dx) % SIDE) * 2 + (c + dc) % 2, (ch + dy) % SIDE)

    def shift(kind, d, k, e):
        return at(e, d, k, 0) if kind == 0 else at(d, e, k, 0)

    far = [(dz, dy) for dz in HOPS for dy in HOPS if (dz, dy) != (0, 0)]
    column = [(0, 0, 0, d) for d in HOPS[:3]]
    peers = {(0, d, k, 0) for d, k in MOVES} | {(d, 0, k, 0) for d, k in MOVES} | set(column)
    barrier = pltpu.get_barrier_semaphore()
    for peer in sorted(peers):
        pl.semaphore_signal(barrier, inc=1, device_id=at(*peer), device_id_type=MESH)

    mine = ((x, z), (z, x))
    incoming = []
    for arr, ref in enumerate((u_ref, g_ref)):
        for step in HOPS:
            for kind in range(2):
                a = (mine[kind][0] + step) % SIDE
                n = len(incoming)
                copy = pltpu.make_async_copy(
                    ref.at[:, pl.ds(pl.multiple_of(kind * 512 + a * 128, 128), 128)], xin.at[n], insem.at[n]
                )
                copy.start()
                incoming.append((copy, step, kind, a, arr))
    table_copies = [pltpu.make_async_copy(h, v, tabsem.at[n]) for n, (h, v) in enumerate(zip(tables_hbm, tables_vmem))]
    for copy in table_copies:
        copy.start()

    def send_a(kind, kh, arr, move):
        d, k = MOVES[move]
        a = mine[kind][0]
        return pltpu.make_async_remote_copy(
            src_ref=turned.at[kind, (a + d) % SIDE, (c + k) % 2, :, kh, arr],
            dst_ref=mid.at[kind, kh, arr, :, a * 2 + c],
            send_sem=s_a.at[kind, kh, arr, move],
            recv_sem=r_a.at[kind, kh, arr, move],
            device_id=shift(kind, d, k, 0),
            device_id_type=MESH,
        )

    def own_a(kind, kh, arr):
        a = mine[kind][0]
        return pltpu.make_async_copy(
            turned.at[kind, a, c, :, kh, arr], mid.at[kind, kh, arr, :, a * 2 + c], l_a.at[kind, kh, arr]
        )

    def send_b(kind, kh, arr, hop):
        b = mine[kind][1]
        return pltpu.make_async_remote_copy(
            src_ref=mid.at[kind, kh, arr, (b + HOPS[hop]) % SIDE],
            dst_ref=land.at[kind, kh, arr, pl.ds(b * 8, 8)],
            send_sem=s_b.at[kind, kh, arr, hop],
            recv_sem=r_b.at[kind, kh, arr, hop],
            device_id=shift(kind, 0, 0, HOPS[hop]),
            device_id_type=MESH,
        )

    def own_b(kind, kh, arr):
        b = mine[kind][1]
        return pltpu.make_async_copy(
            mid.at[kind, kh, arr, b], land.at[kind, kh, arr, pl.ds(b * 8, 8)], l_b.at[kind, kh, arr]
        )

    def turn(n):
        copy, step, kind, a, arr = incoming[n]
        copy.wait()
        turned[kind, a, :, :, :, arr] = xin[n].T.reshape(2, 4, 2, 8, 256)

    def begin(n):
        _, step, kind, a, arr = incoming[n]
        for move, (d, k) in enumerate(MOVES):
            if d == step:
                send_a(kind, 0, arr, move).start()

    early = 4
    for n in range(early):
        turn(n)
    pl.semaphore_wait(barrier, len(peers))
    for n in range(early):
        begin(n)
    for n in range(early, len(incoming)):
        turn(n)
        begin(n)
    for arr in range(2):
        for move in range(len(MOVES)):
            for kind in range(2):
                send_a(kind, 1, arr, move).start()
    for kh in range(2):
        for arr in range(2):
            for kind in range(2):
                own_a(kind, kh, arr).start()
    for peer in column:
        pl.semaphore_signal(far_sem, inc=1, device_id=at(*peer), device_id_type=MESH)

    def find(tile, carry):
        first, second = jnp.int32(0), jnp.int32(0)
        for s in range(32):
            zz, xx, cc = s // 8, (s // 2) % 4, s % 2
            hit = tiles[s] == tile
            first = jnp.where(hit, s, first)
            second = jnp.where(hit, xx * 8 + zz * 2 + cc, second)
        slots[0, tile] = first
        slots[1, tile] = second
        return carry

    lax.fori_loop(0, 32, find, 0)

    def forward(kh, arr):
        for kind in range(2):
            own_a(kind, kh, arr).wait()
            for move in range(len(MOVES)):
                send_a(kind, kh, arr, move).wait_recv()
            for hop in range(3):
                send_b(kind, kh, arr, hop).start()
            own_b(kind, kh, arr).start()

    forward(0, 0)
    for copy in table_copies:
        copy.wait()
    acc_ref[...] = jnp.zeros_like(acc_ref)
    for t in range(32):
        xc, zz = t // 4, t % 4
        block = lags[zz * 8 + xc]
        for half in range(2):
            ends_f[half * 32 + t : half * 32 + t + 1, :] = ends[pl.ds(half * 32 + block, 1), :]
    high, low = split(ends_f[...])
    ends_b[0] = high
    ends_b[1] = low
    forward(0, 1)
    forward(1, 0)
    forward(1, 1)
    inner_table = (fh[...], fl[...])

    def take(kind, kh, arr):
        own_b(kind, kh, arr).wait()
        for hop in range(3):
            send_b(kind, kh, arr, hop).wait_recv()
        stage[...] = land[kind, kh, arr]
        return lambda tile, half: stage[slots[kind, tile], :, half * 128 : half * 128 + 128]

    def spectra(kind, y_ref, part):
        spec_ref[kind, part * 256 : part * 256 + 256] = inner(y_ref, part * 256, inner_table)

    def products(kind, y_ref, part):
        multiply(inner(y_ref, part * 256, inner_table), spec_ref.at[kind], part * 256, acc_ref.at[kind])

    def chunk(kh, carry):
        outer_first(take(0, kh, 0), mid_ref)
        outer_second(twist, mid_ref, y_a)
        load = take(1, kh, 0)
        spectra(0, y_a, 0)
        outer_first(load, mid_ref)
        spectra(0, y_a, 1)
        outer_second(twist, mid_ref, y_b)
        load = take(0, kh, 1)
        spectra(1, y_b, 0)
        outer_first(load, mid_ref)
        spectra(1, y_b, 1)
        outer_second(twist, mid_ref, y_a)
        load = take(1, kh, 1)
        products(0, y_a, 0)
        outer_first(load, mid_ref)
        products(0, y_a, 1)
        outer_second(twist, mid_ref, y_b)
        products(1, y_b, 0)
        products(1, y_b, 1)
        return carry

    lax.fori_loop(0, 2, chunk, 0)

    back = (ih[...], il[...])
    sides = []
    for kind in range(2):
        v = dot3(split(acc_ref[kind]), back)
        re, im = cmul(v[:, 0:128], v[:, 128:256], twist[:, 0:128], twist[:, 128:256])
        sides.append(jnp.concatenate([re, im], axis=0))
    high, low = split(jnp.concatenate(sides, axis=1))
    dot = functools.partial(jnp.dot, preferred_element_type=F32)
    values = dot(ends_b[0], high) + (dot(ends_b[0], low) + dot(ends_b[1], high))

    def send_n(move):
        d, k = MOVES[move]
        return pltpu.make_async_remote_copy(
            src_ref=square,
            dst_ref=near_sq.at[x * 2 + c],
            send_sem=s_n.at[move],
            recv_sem=r_n.at[move],
            device_id=at(0, d, k, 0),
            device_id_type=MESH,
        )

    def send_q(k):
        return pltpu.make_async_remote_copy(
            src_ref=sums,
            dst_ref=tally.at[k],
            send_sem=s_q.at[k],
            recv_sem=r_q.at[k],
            device_id=at(far[k][0], 0, 0, far[k][1]),
            device_id_type=MESH,
        )

    def send_ao(move):
        d, k = MOVES[move]
        return pltpu.make_async_remote_copy(
            src_ref=blocks.at[pl.ds((((x + d) % SIDE) * 2 + (c + k) % 2) * 32, 32)],
            dst_ref=mid_o.at[x * 2 + c],
            send_sem=s_ao.at[move],
            recv_sem=r_ao.at[move],
            device_id=at(0, d, k, 0),
            device_id_type=MESH,
        )

    def send_bo(hop):
        return pltpu.make_async_remote_copy(
            src_ref=mid_o.at[:, pl.ds(((z + HOPS[hop]) % SIDE) * 8, 8)],
            dst_ref=land_o.at[pl.ds(z * 8, 8)],
            send_sem=s_bo.at[hop],
            recv_sem=r_bo.at[hop],
            device_id=at(HOPS[hop], 0, 0, 0),
            device_id_type=MESH,
        )

    both = values[:, 0:128] * values[:, 0:128] + values[:, 128:256] * values[:, 128:256]
    own_square = jnp.sum(both, axis=0, keepdims=True)
    square[...] = own_square
    for move in range(len(MOVES)):
        send_n(move).start()
    for kind in range(2):
        for half in range(2):
            blocks[pl.ds(2 * kind + half, 32, stride=8), :] = values[half * 32 : half * 32 + 32, kind * 128 : kind * 128 + 128]
    for move in range(len(MOVES)):
        send_ao(move).start()
    own_ao = pltpu.make_async_copy(blocks.at[pl.ds((x * 2 + c) * 32, 32)], mid_o.at[x * 2 + c], l_o.at[0])
    own_ao.start()
    near_sq[x * 2 + c] = own_square
    pl.semaphore_wait(far_sem, len(column))
    own_ao.wait()
    for move in range(len(MOVES)):
        send_n(move).wait_recv()
    line_sum = jnp.sum(near_sq[...], axis=0)
    sums[...] = line_sum
    for k in range(len(far)):
        send_q(k).start()
    for move in range(len(MOVES)):
        send_ao(move).wait_recv()
    for hop in range(3):
        send_bo(hop).start()
    own_bo = pltpu.make_async_copy(mid_o.at[:, pl.ds(z * 8, 8)], land_o.at[pl.ds(z * 8, 8)], l_o.at[1])
    own_bo.start()
    for kh in range(2):
        for arr in range(2):
            for kind in range(2):
                for move in range(len(MOVES)):
                    send_a(kind, kh, arr, move).wait_send()
                for hop in range(3):
                    send_b(kind, kh, arr, hop).wait_send()
    for move in range(len(MOVES)):
        send_ao(move).wait_send()
        send_n(move).wait_send()
    own_bo.wait()
    for hop in range(3):
        send_bo(hop).wait_recv()
    rows = land_o.reshape(256, 128)
    for zz in range(4):
        for half in range(2):
            owned[pl.ds(half * 64 + zz, 8, stride=4), :] = rows[pl.ds(zz * 64 + half, 8, stride=8), :]
            for cc in range(2):
                to = half * 64 + 32 + 8 * zz + 4 * cc
                owned[to : to + 4, :] = rows[pl.ds(zz * 64 + cc * 8 + 2 + half, 4, stride=16), :]
    for hop in range(3):
        send_bo(hop).wait_send()
    for k in range(len(far)):
        send_q(k).wait_send()
    for k in range(len(far)):
        send_q(k).wait_recv()
    total = jnp.sum(line_sum + jnp.sum(tally[...], axis=0), axis=1, keepdims=True)
    total_entries = C // GROUP * POS // 2
    factor = target_ratio * math.sqrt(total_entries) / jnp.sqrt(total + epsilon)
    out[:, 0:128] = owned[0:64] * factor
    out[:, 128:256] = owned[64:128] * factor


def shards(inputs, out_grads, tile_order, lag_order):
    vmem = pl.BlockSpec(memory_space=pltpu.VMEM)
    smem = pl.BlockSpec(memory_space=pltpu.SMEM)
    hbm = pl.BlockSpec(memory_space=pl.ANY)
    dma = pltpu.SemaphoreType.DMA
    consts = [jnp.asarray(t) for t in tables()]
    return pl.pallas_call(
        fused_kernel,
        out_shape=jax.ShapeDtypeStruct((64, 256), F32),
        in_specs=[smem, smem] + [hbm] * 8,
        out_specs=vmem,
        scratch_shapes=[pltpu.VMEM(t.shape, t.dtype) for t in consts]
        + [
            pltpu.SMEM((2, 32), jnp.int32),
            pltpu.VMEM((16, 256, 128), F32),
            pltpu.VMEM((2, 4, 2, 4, 2, 2, 8, 256), F32),
            pltpu.VMEM((2, 2, 2, 4, 8, 8, 256), F32),
            pltpu.VMEM((2, 2, 2, 32, 8, 256), F32),
            pltpu.VMEM((32, 8, 256), F32),
            pltpu.VMEM((8, 8, 2, 8, 128), F32),
            pltpu.VMEM((2, ROWS * 8, 256), BF16),
            pltpu.VMEM((2, ROWS * 8, 256), BF16),
            pltpu.VMEM((2, ROWS * 8, 256), F32),
            pltpu.VMEM((2, ROWS, 256), F32),
            pltpu.VMEM((ROWS, 128), F32),
            pltpu.VMEM((2, ROWS, 128), BF16),
            pltpu.VMEM((256, 128), F32),
            pltpu.VMEM((8, 32, 128), F32),
            pltpu.VMEM((32, 8, 128), F32),
            pltpu.VMEM((128, 128), F32),
            pltpu.VMEM((1, 128), F32),
            pltpu.VMEM((8, 1, 128), F32),
            pltpu.VMEM((1, 128), F32),
            pltpu.VMEM((15, 1, 128), F32),
            dma((16,)), dma((6,)), dma((2, 2, 2, 7)), dma((2, 2, 2, 7)), dma((2, 2, 2, 3)), dma((2, 2, 2, 3)),
            dma((2, 2, 2)), dma((2, 2, 2)), dma((7,)), dma((7,)), dma((3,)), dma((3,)), dma((7,)), dma((7,)),
            dma((15,)), dma((15,)), dma((2,)), pltpu.SemaphoreType.REGULAR,
        ],
        compiler_params=pltpu.CompilerParams(collective_id=0, has_side_effects=True),
    )(tile_order, lag_order, inputs, out_grads, *consts)


def solution(mesh):
    return jax.shard_map(
        shards,
        mesh=mesh,
        in_specs=(P("seq", "ch"), P("seq", "ch"), P(), P()),
        out_specs=P("ch", "seq"),
        check_vma=False,
    )
```

```python
import functools
import math

import jax
import jax.numpy as jnp
import numpy as np
from jax import lax
from jax.experimental import pallas as pl
from jax.experimental.pallas import tpu as pltpu
from jax.sharding import PartitionSpec as P

C = 4096
GROUP = 16
target_ratio = 0.5
epsilon = 1e-12

MESH = pl.DeviceIdType.MESH
F32, BF16 = jnp.float32, jnp.bfloat16
SIDE = 4
POS = 16384
ROWS = 64
HOPS = (2, 1, 3, 0)
MOVES = tuple((d, k) for d in HOPS for k in (0, 1) if (d, k) != (0, 0))


def split(values):
    high = values.astype(BF16)
    return high, (values - high.astype(F32)).astype(BF16)


def dot3(left, right):
    dot = functools.partial(jnp.dot, preferred_element_type=F32)
    return dot(left[0], right[0]) + (dot(left[1], right[0]) + dot(left[0], right[1]))


def tables():
    def halves(values):
        high = np.asarray(values, np.float32).astype(jnp.bfloat16)
        return high, (np.asarray(values, np.float32) - high.astype(np.float32)).astype(jnp.bfloat16)

    r = np.arange(128)
    angle = 2 * np.pi * (np.outer(r, r) % 128) / 128
    cos, sin = np.cos(angle), np.sin(angle)
    forward = np.block([[cos, -sin], [sin, cos]])
    inverse = np.block([[cos, sin], [-sin, cos]])
    m, n = np.divmod(np.arange(ROWS), 8)
    odd = 2 * (16 * n + m) + 1
    turn = np.pi * np.outer(odd, r) / POS
    twist = np.concatenate([np.cos(turn), np.sin(turn)], axis=1).astype(np.float32)
    step = 2 * np.arange(32)[None, :] + np.arange(2)[:, None]
    outer = np.pi * (np.outer(step.reshape(-1), odd) % 256) / 128
    ends = np.concatenate([np.cos(outer), -np.sin(outer)], axis=1) / (POS // 2)
    return (*halves(forward), *halves(inverse), twist, ends.astype(np.float32))


def place():
    me = lax.axis_index("seq")
    return me // 8, (me // 2) % 4, me % 2


def cmul(a, b, wr, wi):
    return a * wr - b * wi, a * wi + b * wr


def first_step(x):
    root = math.sqrt(0.5)
    s = [x[p + 4] * root for p in range(4)]
    plus = [x[p] + s[p] for p in range(4)]
    minus = [x[p] - s[p] for p in range(4)]
    out = [None] * 8
    for m in range(4):
        v = []
        for p in range(4):
            re = plus[p] if m in (0, 3) else minus[p]
            im = s[p]
            sign = -1.0 if m in (0, 1) else 1.0
            if p == 0:
                v.append((re, im if sign > 0 else -im))
            else:
                a = math.pi * (2 * m + 1) * p / 16
                wr, wi = math.cos(a), -math.sin(a)
                v.append((re * wr - im * (sign * wi), re * wi + im * (sign * wr)))
        e = (v[0][0] + v[2][0], v[0][1] + v[2][1])
        d = (v[0][0] - v[2][0], v[0][1] - v[2][1])
        f = (v[1][0] + v[3][0], v[1][1] + v[3][1])
        h = (v[1][0] - v[3][0], v[1][1] - v[3][1])
        out[m] = (e[0] + f[0], e[1] + f[1])
        out[m + 4] = (d[0] + h[1], d[1] - h[0])
    return out


def eight(z):
    add = lambda a, b: (a[0] + b[0], a[1] + b[1])
    sub = lambda a, b: (a[0] - b[0], a[1] - b[1])
    turn = lambda a: (a[1], -a[0])

    def four(a, b, c, d):
        e, f, g, h = add(a, c), sub(a, c), add(b, d), turn(sub(b, d))
        return add(e, g), add(f, h), sub(e, g), sub(f, h)

    even, odd = four(z[0], z[2], z[4], z[6]), four(z[1], z[3], z[5], z[7])
    root = math.sqrt(0.5)
    o1 = ((odd[1][0] + odd[1][1]) * root, (odd[1][1] - odd[1][0]) * root)
    o3 = ((odd[3][1] - odd[3][0]) * root, -(odd[3][0] + odd[3][1]) * root)
    turned = (odd[0], o1, turn(odd[2]), o3)
    return [add(even[k], turned[k]) for k in range(4)] + [sub(even[k], turned[k]) for k in range(4)]


def outer_first(load, mid_ref):
    for q2 in range(4):
        for half in range(2):
            out = first_step([load(4 * p + q2, half) for p in range(8)])
            for m in range(8):
                mid_ref[m, 2 * q2 + half, 0] = out[m][0]
                mid_ref[m, 2 * q2 + half, 1] = out[m][1]


def outer_second(twist_ref, mid_ref, y_ref):
    for m in range(8):
        z = []
        for q in range(8):
            re, im = mid_ref[m, q, 0], mid_ref[m, q, 1]
            a = math.pi * (2 * m + 1) * q / 128
            z.append((re, im) if q == 0 else cmul(re, im, math.cos(a), -math.sin(a)))
        done = []
        for n, (re, im) in enumerate(eight(z)):
            row = 8 * m + n
            done.append(cmul(re, im, twist_ref[row : row + 1, 0:128], -twist_ref[row : row + 1, 128:256]))
        for n in range(0, 8, 2):
            for part in range(2):
                pair = split(jnp.concatenate([done[n][part], done[n + 1][part]], axis=0))
                for k in range(2):
                    y_ref[k, (8 * m + n) * 8 : (8 * m + n) * 8 + 16, part * 128 : part * 128 + 128] = pair[k]


def inner(y_ref, at, table):
    return dot3((y_ref[0, at : at + 256], y_ref[1, at : at + 256]), table)


def channel_sums(rows):
    lane = lax.broadcasted_iota(jnp.int32, (8, 128), 0)
    low = lane < 4
    out = []
    for k in range(4):
        a, b = rows[k], rows[k + 4]
        out.append(jnp.where(low, a, b) + pltpu.roll(jnp.where(low, b, a), 4, 0))
    for width in (2, 1):
        keep = lane % (2 * width) < width
        out = [
            jnp.where(keep, a + pltpu.roll(a, 8 - width, 0), b + pltpu.roll(b, width, 0))
            for a, b in zip(out[:width], out[width:])
        ]
    return out[0]


def multiply(grads, spec_ref, at, acc_ref):
    for m in range(4):
        re, im = [], []
        for n in range(8):
            row = m * 64 + n * 8
            gr, gi = grads[row : row + 8, 0:128], grads[row : row + 8, 128:256]
            ur, ui = spec_ref[at + row : at + row + 8, 0:128], spec_ref[at + row : at + row + 8, 128:256]
            re.append(gr * ur + gi * ui)
            im.append(gi * ur - gr * ui)
        to = at // 8 + m * 8
        acc_ref[to : to + 8, 0:128] += channel_sums(re)
        acc_ref[to : to + 8, 128:256] += channel_sums(im)


def fused_kernel(tiles, lags, u_ref, g_ref, *refs):
    tables_hbm, refs = refs[:6], refs[6:]
    out, refs = refs[0], refs[1:]
    tables_vmem, refs = refs[:6], refs[6:]
    fh, fl, ih, il, twist, ends = tables_vmem
    (slots, xin, turned, mid, land, stage, mid_ref, y_a, y_b, spec_ref, acc_ref, ends_f, ends_b, blocks, land_o,
     owned, square, tally,
     insem, tabsem, s_a, r_a, s_b, r_b, l_a, l_b, s_ao, r_ao, s_q, r_q, l_o, line_sem, far_sem) = refs
    z, x, c = place()
    ch = lax.axis_index("ch")

    def at(dz, dx, dc, dy):
        return (((z + dz) % SIDE) * 8 + ((x + dx) % SIDE) * 2 + (c + dc) % 2, (ch + dy) % SIDE)

    def shift(kind, d, k, e):
        return at(e, d, k, 0) if kind == 0 else at(d, e, k, 0)

    others = [(dz, dx, k, dy) for dz in HOPS for dx in HOPS for k in (1, 0) for dy in HOPS]
    others.remove((0, 0, 0, 0))
    others.sort(key=lambda move: -sum(min(d, SIDE - d) for d in (move[0], move[1], move[3])))
    column = [(0, 0, 0, d) for d in HOPS[:3]]
    line = [(d, 0, 0, 0) for d in HOPS[:3]]
    plane = [(dz, dx, k) for dz in HOPS for dx in HOPS for k in (1, 0) if (dz, dx, k) != (0, 0, 0)]
    plane.sort(key=lambda move: -min(move[0], SIDE - move[0]) - min(move[1], SIDE - move[1]))
    peers = {(0, d, k, 0) for d, k in MOVES} | {(d, 0, k, 0) for d, k in MOVES} | set(column)
    barrier = pltpu.get_barrier_semaphore()
    for peer in sorted(peers):
        pl.semaphore_signal(barrier, inc=1, device_id=at(*peer), device_id_type=MESH)

    mine = ((x, z), (z, x))
    incoming = []
    for arr, ref in enumerate((u_ref, g_ref)):
        for step in HOPS:
            for kind in range(2):
                a = (mine[kind][0] + step) % SIDE
                n = len(incoming)
                copy = pltpu.make_async_copy(
                    ref.at[:, pl.ds(pl.multiple_of(kind * 512 + a * 128, 128), 128)], xin.at[n], insem.at[n]
                )
                copy.start()
                incoming.append((copy, step, kind, a, arr))
    table_copies = [pltpu.make_async_copy(h, v, tabsem.at[n]) for n, (h, v) in enumerate(zip(tables_hbm, tables_vmem))]
    for copy in table_copies:
        copy.start()

    def send_a(kind, kh, arr, move):
        d, k = MOVES[move]
        a = mine[kind][0]
        return pltpu.make_async_remote_copy(
            src_ref=turned.at[kind, (a + d) % SIDE, (c + k) % 2, :, kh, arr],
            dst_ref=mid.at[kind, kh, arr, :, a * 2 + c],
            send_sem=s_a.at[kind, kh, arr, move],
            recv_sem=r_a.at[kind, kh, arr, move],
            device_id=shift(kind, d, k, 0),
            device_id_type=MESH,
        )

    def own_a(kind, kh, arr):
        a = mine[kind][0]
        return pltpu.make_async_copy(
            turned.at[kind, a, c, :, kh, arr], mid.at[kind, kh, arr, :, a * 2 + c], l_a.at[kind, kh, arr]
        )

    def send_b(kind, kh, arr, hop):
        b = mine[kind][1]
        return pltpu.make_async_remote_copy(
            src_ref=mid.at[kind, kh, arr, (b + HOPS[hop]) % SIDE],
            dst_ref=land.at[kind, kh, arr, pl.ds(b * 8, 8)],
            send_sem=s_b.at[kind, kh, arr, hop],
            recv_sem=r_b.at[kind, kh, arr, hop],
            device_id=shift(kind, 0, 0, HOPS[hop]),
            device_id_type=MESH,
        )

    def own_b(kind, kh, arr):
        b = mine[kind][1]
        return pltpu.make_async_copy(
            mid.at[kind, kh, arr, b], land.at[kind, kh, arr, pl.ds(b * 8, 8)], l_b.at[kind, kh, arr]
        )

    def turn(n):
        copy, step, kind, a, arr = incoming[n]
        copy.wait()
        turned[kind, a, :, :, :, arr] = xin[n].T.reshape(2, 4, 2, 8, 256)

    def begin(n):
        _, step, kind, a, arr = incoming[n]
        for move, (d, k) in enumerate(MOVES):
            if d == step:
                send_a(kind, 0, arr, move).start()

    early = 4
    for n in range(early):
        turn(n)
    pl.semaphore_wait(barrier, len(peers))
    for n in range(early):
        begin(n)
    for n in range(early, len(incoming)):
        turn(n)
        begin(n)
    for arr in range(2):
        for move in range(len(MOVES)):
            for kind in range(2):
                send_a(kind, 1, arr, move).start()
    for kh in range(2):
        for arr in range(2):
            for kind in range(2):
                own_a(kind, kh, arr).start()
    for peer in line:
        pl.semaphore_signal(line_sem, inc=1, device_id=at(*peer), device_id_type=MESH)

    def find(tile, carry):
        first, second = jnp.int32(0), jnp.int32(0)
        for s in range(32):
            zz, xx, cc = s // 8, (s // 2) % 4, s % 2
            hit = tiles[s] == tile
            first = jnp.where(hit, s, first)
            second = jnp.where(hit, xx * 8 + zz * 2 + cc, second)
        slots[0, tile] = first
        slots[1, tile] = second
        return carry

    lax.fori_loop(0, 32, find, 0)

    def forward(kh, arr):
        for kind in range(2):
            own_a(kind, kh, arr).wait()
            for move in range(len(MOVES)):
                send_a(kind, kh, arr, move).wait_recv()
            for hop in range(3):
                send_b(kind, kh, arr, hop).start()
            own_b(kind, kh, arr).start()

    pl.semaphore_wait(line_sem, len(line))
    for peer in column:
        pl.semaphore_signal(far_sem, inc=1, device_id=at(*peer), device_id_type=MESH)
    forward(0, 0)
    for copy in table_copies:
        copy.wait()
    acc_ref[...] = jnp.zeros_like(acc_ref)
    for t in range(32):
        xc, zz = t // 4, t % 4
        block = lags[zz * 8 + xc]
        for half in range(2):
            ends_f[half * 32 + t : half * 32 + t + 1, :] = ends[pl.ds(half * 32 + block, 1), :]
    high, low = split(ends_f[...])
    ends_b[0] = high
    ends_b[1] = low
    forward(0, 1)
    forward(1, 0)
    forward(1, 1)
    inner_table = (fh[...], fl[...])

    def take(kind, kh, arr):
        own_b(kind, kh, arr).wait()
        for hop in range(3):
            send_b(kind, kh, arr, hop).wait_recv()
        stage[...] = land[kind, kh, arr]
        return lambda tile, half: stage[slots[kind, tile], :, half * 128 : half * 128 + 128]

    def spectra(kind, y_ref, part):
        spec_ref[kind, part * 256 : part * 256 + 256] = inner(y_ref, part * 256, inner_table)

    def products(kind, y_ref, part):
        multiply(inner(y_ref, part * 256, inner_table), spec_ref.at[kind], part * 256, acc_ref.at[kind])

    def chunk(kh, carry):
        outer_first(take(0, kh, 0), mid_ref)
        outer_second(twist, mid_ref, y_a)
        load = take(1, kh, 0)
        spectra(0, y_a, 0)
        outer_first(load, mid_ref)
        spectra(0, y_a, 1)
        outer_second(twist, mid_ref, y_b)
        load = take(0, kh, 1)
        spectra(1, y_b, 0)
        outer_first(load, mid_ref)
        spectra(1, y_b, 1)
        outer_second(twist, mid_ref, y_a)
        load = take(1, kh, 1)
        products(0, y_a, 0)
        outer_first(load, mid_ref)
        products(0, y_a, 1)
        outer_second(twist, mid_ref, y_b)
        products(1, y_b, 0)
        products(1, y_b, 1)
        return carry

    lax.fori_loop(0, 2, chunk, 0)

    back = (ih[...], il[...])
    sides = []
    for kind in range(2):
        v = dot3(split(acc_ref[kind]), back)
        re, im = cmul(v[:, 0:128], v[:, 128:256], twist[:, 0:128], twist[:, 128:256])
        sides.append(jnp.concatenate([re, im], axis=0))
    high, low = split(jnp.concatenate(sides, axis=1))
    dot = functools.partial(jnp.dot, preferred_element_type=F32)
    values = dot(ends_b[0], high) + (dot(ends_b[0], low) + dot(ends_b[1], high))

    def send_q(k):
        return pltpu.make_async_remote_copy(
            src_ref=square, dst_ref=tally.at[k], send_sem=s_q, recv_sem=r_q, device_id=at(*others[k]), device_id_type=MESH
        )

    every_q = pltpu.make_async_remote_copy(
        src_ref=tally, dst_ref=tally, send_sem=s_q, recv_sem=r_q, device_id=at(*others[0]), device_id_type=MESH
    )

    def send_ao(move):
        dz, dx, k = plane[move]
        to = (((x + dx) % SIDE) * 2 + (c + k) % 2) * 4 + (z + dz) % SIDE
        return pltpu.make_async_remote_copy(
            src_ref=blocks.at[pl.ds(to * 8, 8)],
            dst_ref=land_o.at[z * 8 + x * 2 + c],
            send_sem=s_ao.at[move],
            recv_sem=r_ao.at[move],
            device_id=at(dz, dx, k, 0),
            device_id_type=MESH,
        )

    both = values[:, 0:128] * values[:, 0:128] + values[:, 128:256] * values[:, 128:256]
    own_square = jnp.sum(both, axis=0, keepdims=True)
    square[...] = own_square
    pl.semaphore_wait(far_sem, len(column))
    for k in range(len(others)):
        send_q(k).start()
    for kind in range(2):
        for half in range(2):
            blocks[pl.ds(2 * kind + half, 32, stride=8), :] = values[half * 32 : half * 32 + 32, kind * 128 : kind * 128 + 128]
    for move in range(len(plane)):
        send_ao(move).start()
    own_ao = pltpu.make_async_copy(blocks.at[pl.ds(((x * 2 + c) * 4 + z) * 8, 8)], land_o.at[z * 8 + x * 2 + c], l_o)
    own_ao.start()
    for kh in range(2):
        for arr in range(2):
            for kind in range(2):
                for move in range(len(MOVES)):
                    send_a(kind, kh, arr, move).wait_send()
                for hop in range(3):
                    send_b(kind, kh, arr, hop).wait_send()
    own_ao.wait()
    for move in range(len(plane)):
        send_ao(move).wait()
    rows = land_o.reshape(256, 128)
    for zz in range(4):
        for half in range(2):
            owned[pl.ds(half * 64 + zz, 8, stride=4), :] = rows[pl.ds(zz * 64 + half, 8, stride=8), :]
            for cc in range(2):
                to = half * 64 + 32 + 8 * zz + 4 * cc
                owned[to : to + 4, :] = rows[pl.ds(zz * 64 + cc * 8 + 2 + half, 4, stride=16), :]
    every_q.wait_send()
    every_q.wait_recv()
    total = jnp.sum(own_square + jnp.sum(tally[...], axis=0), axis=1, keepdims=True)
    total_entries = C // GROUP * POS // 2
    factor = target_ratio * math.sqrt(total_entries) / jnp.sqrt(total + epsilon)
    out[:, 0:128] = owned[0:64] * factor
    out[:, 128:256] = owned[64:128] * factor


def shards(inputs, out_grads, tile_order, lag_order):
    vmem = pl.BlockSpec(memory_space=pltpu.VMEM)
    smem = pl.BlockSpec(memory_space=pltpu.SMEM)
    hbm = pl.BlockSpec(memory_space=pl.ANY)
    dma = pltpu.SemaphoreType.DMA
    consts = [jnp.asarray(t) for t in tables()]
    return pl.pallas_call(
        fused_kernel,
        out_shape=pltpu.VMEM((64, 256), F32),
        in_specs=[smem, smem] + [hbm] * 8,
        out_specs=vmem,
        scratch_shapes=[pltpu.VMEM(t.shape, t.dtype) for t in consts]
        + [
            pltpu.SMEM((2, 32), jnp.int32),
            pltpu.VMEM((16, 256, 128), F32),
            pltpu.VMEM((2, 4, 2, 4, 2, 2, 8, 256), F32),
            pltpu.VMEM((2, 2, 2, 4, 8, 8, 256), F32),
            pltpu.VMEM((2, 2, 2, 32, 8, 256), F32),
            pltpu.VMEM((32, 8, 256), F32),
            pltpu.VMEM((8, 8, 2, 8, 128), F32),
            pltpu.VMEM((2, ROWS * 8, 256), BF16),
            pltpu.VMEM((2, ROWS * 8, 256), BF16),
            pltpu.VMEM((2, ROWS * 8, 256), F32),
            pltpu.VMEM((2, ROWS, 256), F32),
            pltpu.VMEM((ROWS, 128), F32),
            pltpu.VMEM((2, ROWS, 128), BF16),
            pltpu.VMEM((256, 128), F32),
            pltpu.VMEM((32, 8, 128), F32),
            pltpu.VMEM((128, 128), F32),
            pltpu.VMEM((1, 128), F32),
            pltpu.VMEM((127, 1, 128), F32),
            dma((16,)), dma((6,)), dma((2, 2, 2, 7)), dma((2, 2, 2, 7)), dma((2, 2, 2, 3)), dma((2, 2, 2, 3)),
            dma((2, 2, 2)), dma((2, 2, 2)), dma((31,)), dma((31,)), dma, dma, dma, pltpu.SemaphoreType.REGULAR, pltpu.SemaphoreType.REGULAR,
        ],
        compiler_params=pltpu.CompilerParams(collective_id=0, has_side_effects=True),
    )(tile_order, lag_order, inputs, out_grads, *consts)


def solution(mesh):
    return jax.shard_map(
        shards,
        mesh=mesh,
        in_specs=(P("seq", "ch"), P("seq", "ch"), P(), P()),
        out_specs=P("ch", "seq"),
        check_vma=False,
    )
```

```python
import functools
import math

import jax
import jax.numpy as jnp
import numpy as np
from jax import lax
from jax.experimental import pallas as pl
from jax.experimental.pallas import tpu as pltpu
from jax.sharding import PartitionSpec as P

C = 4096
GROUP = 16
target_ratio = 0.5
epsilon = 1e-12

MESH = pl.DeviceIdType.MESH
F32, BF16 = jnp.float32, jnp.bfloat16
SIDE = 4
POS = 16384
ROWS = 64
HOPS = (2, 1, 3, 0)
MOVES = tuple((d, k) for d in HOPS for k in (0, 1) if (d, k) != (0, 0))


def split(values):
    high = values.astype(BF16)
    return high, (values - high.astype(F32)).astype(BF16)


def dot3(left, right):
    dot = functools.partial(jnp.dot, preferred_element_type=F32)
    return dot(left[0], right[0]) + (dot(left[1], right[0]) + dot(left[0], right[1]))


def tables():
    def halves(values):
        high = np.asarray(values, np.float32).astype(jnp.bfloat16)
        return high, (np.asarray(values, np.float32) - high.astype(np.float32)).astype(jnp.bfloat16)

    r = np.arange(128)
    angle = 2 * np.pi * (np.outer(r, r) % 128) / 128
    cos, sin = np.cos(angle), np.sin(angle)
    forward = np.block([[cos, -sin], [sin, cos]])
    inverse = np.block([[cos, sin], [-sin, cos]])
    m, n = np.divmod(np.arange(ROWS), 8)
    odd = 2 * (16 * n + m) + 1
    turn = np.pi * np.outer(odd, r) / POS
    twist = np.concatenate([np.cos(turn), np.sin(turn)], axis=1).astype(np.float32)
    step = 2 * np.arange(32)[None, :] + np.arange(2)[:, None]
    outer = np.pi * (np.outer(step.reshape(-1), odd) % 256) / 128
    ends = np.concatenate([np.cos(outer), -np.sin(outer)], axis=1) / (POS // 2)
    return (*halves(forward), *halves(inverse), twist, ends.astype(np.float32))


def place():
    me = lax.axis_index("seq")
    return me // 8, (me // 2) % 4, me % 2


def cmul(a, b, wr, wi):
    return a * wr - b * wi, a * wi + b * wr


def first_step(x):
    root = math.sqrt(0.5)
    s = [x[p + 4] * root for p in range(4)]
    plus = [x[p] + s[p] for p in range(4)]
    minus = [x[p] - s[p] for p in range(4)]
    out = [None] * 8
    for m in range(4):
        v = []
        for p in range(4):
            re = plus[p] if m in (0, 3) else minus[p]
            im = s[p]
            sign = -1.0 if m in (0, 1) else 1.0
            if p == 0:
                v.append((re, im if sign > 0 else -im))
            else:
                a = math.pi * (2 * m + 1) * p / 16
                wr, wi = math.cos(a), -math.sin(a)
                v.append((re * wr - im * (sign * wi), re * wi + im * (sign * wr)))
        e = (v[0][0] + v[2][0], v[0][1] + v[2][1])
        d = (v[0][0] - v[2][0], v[0][1] - v[2][1])
        f = (v[1][0] + v[3][0], v[1][1] + v[3][1])
        h = (v[1][0] - v[3][0], v[1][1] - v[3][1])
        out[m] = (e[0] + f[0], e[1] + f[1])
        out[m + 4] = (d[0] + h[1], d[1] - h[0])
    return out


def eight(z):
    add = lambda a, b: (a[0] + b[0], a[1] + b[1])
    sub = lambda a, b: (a[0] - b[0], a[1] - b[1])
    turn = lambda a: (a[1], -a[0])

    def four(a, b, c, d):
        e, f, g, h = add(a, c), sub(a, c), add(b, d), turn(sub(b, d))
        return add(e, g), add(f, h), sub(e, g), sub(f, h)

    even, odd = four(z[0], z[2], z[4], z[6]), four(z[1], z[3], z[5], z[7])
    root = math.sqrt(0.5)
    o1 = ((odd[1][0] + odd[1][1]) * root, (odd[1][1] - odd[1][0]) * root)
    o3 = ((odd[3][1] - odd[3][0]) * root, -(odd[3][0] + odd[3][1]) * root)
    turned = (odd[0], o1, turn(odd[2]), o3)
    return [add(even[k], turned[k]) for k in range(4)] + [sub(even[k], turned[k]) for k in range(4)]


def outer_first(load, mid_ref):
    for q2 in range(4):
        for half in range(2):
            out = first_step([load(4 * p + q2, half) for p in range(8)])
            for m in range(8):
                mid_ref[m, 2 * q2 + half, 0] = out[m][0]
                mid_ref[m, 2 * q2 + half, 1] = out[m][1]


def outer_second(twist_ref, mid_ref, y_ref):
    for m in range(8):
        z = []
        for q in range(8):
            re, im = mid_ref[m, q, 0], mid_ref[m, q, 1]
            a = math.pi * (2 * m + 1) * q / 128
            z.append((re, im) if q == 0 else cmul(re, im, math.cos(a), -math.sin(a)))
        done = []
        for n, (re, im) in enumerate(eight(z)):
            row = 8 * m + n
            done.append(cmul(re, im, twist_ref[row : row + 1, 0:128], -twist_ref[row : row + 1, 128:256]))
        for n in range(0, 8, 2):
            for part in range(2):
                pair = split(jnp.concatenate([done[n][part], done[n + 1][part]], axis=0))
                for k in range(2):
                    y_ref[k, (8 * m + n) * 8 : (8 * m + n) * 8 + 16, part * 128 : part * 128 + 128] = pair[k]


def inner(y_ref, at, table):
    return dot3((y_ref[0], y_ref[1]), table)


def channel_sums(rows):
    lane = lax.broadcasted_iota(jnp.int32, (8, 128), 0)
    low = lane < 4
    out = []
    for k in range(4):
        a, b = rows[k], rows[k + 4]
        out.append(jnp.where(low, a, b) + pltpu.roll(jnp.where(low, b, a), 4, 0))
    for width in (2, 1):
        keep = lane % (2 * width) < width
        out = [
            jnp.where(keep, a + pltpu.roll(a, 8 - width, 0), b + pltpu.roll(b, width, 0))
            for a, b in zip(out[:width], out[width:])
        ]
    return out[0]


def multiply(grads, spec_ref, at, acc_ref):
    for m in range(8):
        re, im = [], []
        for n in range(8):
            row = m * 64 + n * 8
            gr, gi = grads[row : row + 8, 0:128], grads[row : row + 8, 128:256]
            ur, ui = spec_ref[at + row : at + row + 8, 0:128], spec_ref[at + row : at + row + 8, 128:256]
            re.append(gr * ur + gi * ui)
            im.append(gi * ur - gr * ui)
        to = at // 8 + m * 8
        acc_ref[to : to + 8, 0:128] += channel_sums(re)
        acc_ref[to : to + 8, 128:256] += channel_sums(im)


def fused_kernel(tiles_hbm, lags_hbm, u_ref, g_ref, *refs):
    tables_hbm, refs = refs[:6], refs[6:]
    out, refs = refs[0], refs[1:]
    tables_vmem, refs = refs[:6], refs[6:]
    fh, fl, ih, il, twist, ends = tables_vmem
    (tiles, lags, slots, xin, turned, mid, land, stage, mid_ref, y_a, y_b, spec_ref, acc_ref, ends_f, ends_b, blocks, land_o,
     owned, square, tally,
     insem, ordsem, tabsem, s_a, r_a, s_b, r_b, l_a, l_b, s_ao, r_ao, s_q, r_q, l_o, line_sem, far_sem) = refs
    z, x, c = place()
    ch = lax.axis_index("ch")

    def at(dz, dx, dc, dy):
        return (((z + dz) % SIDE) * 8 + ((x + dx) % SIDE) * 2 + (c + dc) % 2, (ch + dy) % SIDE)

    def shift(kind, d, k, e):
        return at(e, d, k, 0) if kind == 0 else at(d, e, k, 0)

    others = [(dz, dx, k, dy) for dz in HOPS for dx in HOPS for k in (1, 0) for dy in HOPS]
    others.remove((0, 0, 0, 0))
    others.sort(key=lambda move: -sum(min(d, SIDE - d) for d in (move[0], move[1], move[3])))
    column = [(0, 0, 0, d) for d in HOPS[:3]]
    line = [(d, 0, 0, 0) for d in HOPS[:3]]
    plane = [(dz, dx, k) for dz in HOPS for dx in HOPS for k in (1, 0) if (dz, dx, k) != (0, 0, 0)]
    plane.sort(key=lambda move: -min(move[0], SIDE - move[0]) - min(move[1], SIDE - move[1]))
    peers = {(0, d, k, 0) for d, k in MOVES} | {(d, 0, k, 0) for d, k in MOVES} | set(column)
    barrier = pltpu.get_barrier_semaphore()
    for peer in sorted(peers):
        pl.semaphore_signal(barrier, inc=1, device_id=at(*peer), device_id_type=MESH)

    mine = ((x, z), (z, x))
    incoming = []
    for arr, ref in enumerate((u_ref, g_ref)):
        for step in HOPS:
            for kind in range(2):
                a = (mine[kind][0] + step) % SIDE
                n = len(incoming)
                copy = pltpu.make_async_copy(
                    ref.at[:, pl.ds(pl.multiple_of(kind * 512 + a * 128, 128), 128)], xin.at[n], insem.at[n]
                )
                copy.start()
                incoming.append((copy, step, kind, a, arr))
    order_copies = [
        pltpu.make_async_copy(tiles_hbm, tiles, ordsem.at[0]),
        pltpu.make_async_copy(lags_hbm, lags, ordsem.at[1]),
    ]
    for copy in order_copies:
        copy.start()
    table_copies = [pltpu.make_async_copy(h, v, tabsem.at[n]) for n, (h, v) in enumerate(zip(tables_hbm, tables_vmem))]
    for copy in table_copies:
        copy.start()

    def send_a(kind, kh, arr, move):
        d, k = MOVES[move]
        a = mine[kind][0]
        return pltpu.make_async_remote_copy(
            src_ref=turned.at[kind, (a + d) % SIDE, (c + k) % 2, :, kh, arr],
            dst_ref=mid.at[kind, kh, arr, :, a * 2 + c],
            send_sem=s_a.at[kind, kh, arr, move],
            recv_sem=r_a.at[kind, kh, arr, move],
            device_id=shift(kind, d, k, 0),
            device_id_type=MESH,
        )

    def own_a(kind, kh, arr):
        a = mine[kind][0]
        return pltpu.make_async_copy(
            turned.at[kind, a, c, :, kh, arr], mid.at[kind, kh, arr, :, a * 2 + c], l_a.at[kind, kh, arr]
        )

    def send_b(kind, kh, arr, hop):
        b = mine[kind][1]
        return pltpu.make_async_remote_copy(
            src_ref=mid.at[kind, kh, arr, (b + HOPS[hop]) % SIDE],
            dst_ref=land.at[kind, kh, arr, pl.ds(b * 8, 8)],
            send_sem=s_b.at[kind, kh, arr, hop],
            recv_sem=r_b.at[kind, kh, arr, hop],
            device_id=shift(kind, 0, 0, HOPS[hop]),
            device_id_type=MESH,
        )

    def own_b(kind, kh, arr):
        b = mine[kind][1]
        return pltpu.make_async_copy(
            mid.at[kind, kh, arr, b], land.at[kind, kh, arr, pl.ds(b * 8, 8)], l_b.at[kind, kh, arr]
        )

    def turn(n):
        copy, step, kind, a, arr = incoming[n]
        copy.wait()
        turned[kind, a, :, :, :, arr] = xin[n].T.reshape(2, 4, 2, 8, 256)

    def begin(n):
        _, step, kind, a, arr = incoming[n]
        for move, (d, k) in enumerate(MOVES):
            if d == step:
                send_a(kind, 0, arr, move).start()

    early = 4
    for n in range(early):
        turn(n)
    pl.semaphore_wait(barrier, len(peers))
    for n in range(early):
        begin(n)
    for n in range(early, len(incoming)):
        turn(n)
        begin(n)
    for arr in range(2):
        for move in range(len(MOVES)):
            for kind in range(2):
                send_a(kind, 1, arr, move).start()
    for kh in range(2):
        for arr in range(2):
            for kind in range(2):
                own_a(kind, kh, arr).start()
    for peer in line:
        pl.semaphore_signal(line_sem, inc=1, device_id=at(*peer), device_id_type=MESH)

    for copy in order_copies:
        copy.wait()

    def find(tile, carry):
        first, second = jnp.int32(0), jnp.int32(0)
        for s in range(32):
            zz, xx, cc = s // 8, (s // 2) % 4, s % 2
            hit = tiles[s] == tile
            first = jnp.where(hit, s, first)
            second = jnp.where(hit, xx * 8 + zz * 2 + cc, second)
        slots[0, tile] = first
        slots[1, tile] = second
        return carry

    lax.fori_loop(0, 32, find, 0)

    def forward(kh, arr):
        for kind in range(2):
            own_a(kind, kh, arr).wait()
            for move in range(len(MOVES)):
                send_a(kind, kh, arr, move).wait_recv()
            for hop in range(3):
                send_b(kind, kh, arr, hop).start()
            own_b(kind, kh, arr).start()

    pl.semaphore_wait(line_sem, len(line))
    for peer in column:
        pl.semaphore_signal(far_sem, inc=1, device_id=at(*peer), device_id_type=MESH)
    forward(0, 0)
    for copy in table_copies:
        copy.wait()
    acc_ref[...] = jnp.zeros_like(acc_ref)
    for t in range(32):
        xc, zz = t // 4, t % 4
        block = lags[zz * 8 + xc]
        for half in range(2):
            ends_f[half * 32 + t : half * 32 + t + 1, :] = ends[pl.ds(half * 32 + block, 1), :]
    high, low = split(ends_f[...])
    ends_b[0] = high
    ends_b[1] = low
    forward(0, 1)
    forward(1, 0)
    forward(1, 1)
    inner_table = (fh[...], fl[...])

    def take(kind, kh, arr):
        own_b(kind, kh, arr).wait()
        for hop in range(3):
            send_b(kind, kh, arr, hop).wait_recv()
        stage[...] = land[kind, kh, arr]
        return lambda tile, half: stage[slots[kind, tile], :, half * 128 : half * 128 + 128]

    def spectra(kind, y_ref, part):
        spec_ref[kind] = inner(y_ref, part * 256, inner_table)

    def products(kind, y_ref, part):
        multiply(inner(y_ref, part * 256, inner_table), spec_ref.at[kind], part * 256, acc_ref.at[kind])

    def chunk(kh, carry):
        outer_first(take(0, kh, 0), mid_ref)
        outer_second(twist, mid_ref, y_a)
        load = take(1, kh, 0)
        spectra(0, y_a, 0)
        outer_first(load, mid_ref)
        outer_second(twist, mid_ref, y_b)
        spectra(1, y_b, 0)
        outer_first(take(0, kh, 1), mid_ref)
        outer_second(twist, mid_ref, y_a)
        load = take(1, kh, 1)
        products(0, y_a, 0)
        outer_first(load, mid_ref)
        outer_second(twist, mid_ref, y_b)
        products(1, y_b, 0)
        return carry

    lax.fori_loop(0, 2, chunk, 0)

    back = (ih[...], il[...])
    sides = []
    for kind in range(2):
        v = dot3(split(acc_ref[kind]), back)
        re, im = cmul(v[:, 0:128], v[:, 128:256], twist[:, 0:128], twist[:, 128:256])
        sides.append(jnp.concatenate([re, im], axis=0))
    high, low = split(jnp.concatenate(sides, axis=1))
    dot = functools.partial(jnp.dot, preferred_element_type=F32)
    values = dot(ends_b[0], high) + (dot(ends_b[0], low) + dot(ends_b[1], high))

    def send_q(k):
        return pltpu.make_async_remote_copy(
            src_ref=square, dst_ref=tally.at[k], send_sem=s_q, recv_sem=r_q, device_id=at(*others[k]), device_id_type=MESH
        )

    every_q = pltpu.make_async_remote_copy(
        src_ref=tally, dst_ref=tally, send_sem=s_q, recv_sem=r_q, device_id=at(*others[0]), device_id_type=MESH
    )

    def send_ao(move):
        dz, dx, k = plane[move]
        to = (((x + dx) % SIDE) * 2 + (c + k) % 2) * 4 + (z + dz) % SIDE
        return pltpu.make_async_remote_copy(
            src_ref=blocks.at[pl.ds(to * 8, 8)],
            dst_ref=land_o.at[z * 8 + x * 2 + c],
            send_sem=s_ao.at[move],
            recv_sem=r_ao.at[move],
            device_id=at(dz, dx, k, 0),
            device_id_type=MESH,
        )

    both = values[:, 0:128] * values[:, 0:128] + values[:, 128:256] * values[:, 128:256]
    own_square = jnp.sum(both, axis=0, keepdims=True)
    square[...] = own_square
    pl.semaphore_wait(far_sem, len(column))
    for k in range(len(others)):
        send_q(k).start()
    for kind in range(2):
        for half in range(2):
            blocks[pl.ds(2 * kind + half, 32, stride=8), :] = values[half * 32 : half * 32 + 32, kind * 128 : kind * 128 + 128]
    for move in range(len(plane)):
        send_ao(move).start()
    own_ao = pltpu.make_async_copy(blocks.at[pl.ds(((x * 2 + c) * 4 + z) * 8, 8)], land_o.at[z * 8 + x * 2 + c], l_o)
    own_ao.start()
    for kh in range(2):
        for arr in range(2):
            for kind in range(2):
                for move in range(len(MOVES)):
                    send_a(kind, kh, arr, move).wait_send()
                for hop in range(3):
                    send_b(kind, kh, arr, hop).wait_send()
    own_ao.wait()
    for move in range(len(plane)):
        send_ao(move).wait()
    rows = land_o.reshape(256, 128)
    for zz in range(4):
        for half in range(2):
            owned[pl.ds(half * 64 + zz, 8, stride=4), :] = rows[pl.ds(zz * 64 + half, 8, stride=8), :]
            for cc in range(2):
                to = half * 64 + 32 + 8 * zz + 4 * cc
                owned[to : to + 4, :] = rows[pl.ds(zz * 64 + cc * 8 + 2 + half, 4, stride=16), :]
    every_q.wait_send()
    every_q.wait_recv()
    total = jnp.sum(own_square + jnp.sum(tally[...], axis=0), axis=1, keepdims=True)
    total_entries = C // GROUP * POS // 2
    factor = target_ratio * math.sqrt(total_entries) / jnp.sqrt(total + epsilon)
    out[:, 0:128] = owned[0:64] * factor
    out[:, 128:256] = owned[64:128] * factor


def shards(inputs, out_grads, tile_order, lag_order):
    vmem = pl.BlockSpec(memory_space=pltpu.VMEM)
    hbm = pl.BlockSpec(memory_space=pl.ANY)
    dma = pltpu.SemaphoreType.DMA
    consts = [jnp.asarray(t) for t in tables()]
    return pl.pallas_call(
        fused_kernel,
        out_shape=pltpu.VMEM((64, 256), F32),
        in_specs=[hbm] * 10,
        out_specs=vmem,
        scratch_shapes=[pltpu.VMEM(t.shape, t.dtype) for t in consts]
        + [
            pltpu.SMEM((32,), jnp.int32),
            pltpu.SMEM((32,), jnp.int32),
            pltpu.SMEM((2, 32), jnp.int32),
            pltpu.VMEM((16, 256, 128), F32),
            pltpu.VMEM((2, 4, 2, 4, 2, 2, 8, 256), F32),
            pltpu.VMEM((2, 2, 2, 4, 8, 8, 256), F32),
            pltpu.VMEM((2, 2, 2, 32, 8, 256), F32),
            pltpu.VMEM((32, 8, 256), F32),
            pltpu.VMEM((8, 8, 2, 8, 128), F32),
            pltpu.VMEM((2, ROWS * 8, 256), BF16),
            pltpu.VMEM((2, ROWS * 8, 256), BF16),
            pltpu.VMEM((2, ROWS * 8, 256), F32),
            pltpu.VMEM((2, ROWS, 256), F32),
            pltpu.VMEM((ROWS, 128), F32),
            pltpu.VMEM((2, ROWS, 128), BF16),
            pltpu.VMEM((256, 128), F32),
            pltpu.VMEM((32, 8, 128), F32),
            pltpu.VMEM((128, 128), F32),
            pltpu.VMEM((1, 128), F32),
            pltpu.VMEM((127, 1, 128), F32),
            dma((16,)), dma((2,)), dma((6,)), dma((2, 2, 2, 7)), dma((2, 2, 2, 7)), dma((2, 2, 2, 3)), dma((2, 2, 2, 3)),
            dma((2, 2, 2)), dma((2, 2, 2)), dma((31,)), dma((31,)), dma, dma, dma, pltpu.SemaphoreType.REGULAR, pltpu.SemaphoreType.REGULAR,
        ],
        compiler_params=pltpu.CompilerParams(collective_id=0, has_side_effects=True),
    )(tile_order, lag_order, inputs, out_grads, *consts)


def solution(mesh):
    return jax.shard_map(
        shards,
        mesh=mesh,
        in_specs=(P("seq", "ch"), P("seq", "ch"), P(), P()),
        out_specs=P("ch", "seq"),
        check_vma=False,
    )
```

```python
import functools
import math

import jax
import jax.numpy as jnp
import numpy as np
from jax import lax
from jax.experimental import pallas as pl
from jax.experimental.pallas import tpu as pltpu
from jax.sharding import PartitionSpec as P

C = 4096
GROUP = 16
target_ratio = 0.5
epsilon = 1e-12

MESH = pl.DeviceIdType.MESH
F32, BF16 = jnp.float32, jnp.bfloat16
SIDE = 4
POS = 16384
ROWS = 64
PARTS = 4
PART = ROWS * 8 // PARTS
HOPS = (2, 1, 3, 0)
MOVES = tuple((d, k) for d in HOPS for k in (0, 1) if (d, k) != (0, 0))


def split(values):
    high = values.astype(BF16)
    return high, (values - high.astype(F32)).astype(BF16)


def dot3(left, right):
    dot = functools.partial(jnp.dot, preferred_element_type=F32)
    return dot(left[0], right[0]) + (dot(left[1], right[0]) + dot(left[0], right[1]))


def tables():
    def halves(values):
        high = np.asarray(values, np.float32).astype(jnp.bfloat16)
        return high, (np.asarray(values, np.float32) - high.astype(np.float32)).astype(jnp.bfloat16)

    r = np.arange(128)
    angle = 2 * np.pi * (np.outer(r, r) % 128) / 128
    cos, sin = np.cos(angle), np.sin(angle)
    forward = np.block([[cos, -sin], [sin, cos]])
    inverse = np.block([[cos, sin], [-sin, cos]])
    m, n = np.divmod(np.arange(ROWS), 8)
    odd = 2 * (16 * n + m) + 1
    turn = np.pi * np.outer(odd, r) / POS
    twist = np.concatenate([np.cos(turn), np.sin(turn)], axis=1).astype(np.float32)
    step = 2 * np.arange(32)[None, :] + np.arange(2)[:, None]
    outer = np.pi * (np.outer(step.reshape(-1), odd) % 256) / 128
    ends = np.concatenate([np.cos(outer), -np.sin(outer)], axis=1) / (POS // 2)
    return (*halves(forward), *halves(inverse), twist, ends.astype(np.float32))


def place():
    me = lax.axis_index("seq")
    return me // 8, (me // 2) % 4, me % 2


def cmul(a, b, wr, wi):
    return a * wr - b * wi, a * wi + b * wr


def first_step(x):
    root = math.sqrt(0.5)
    s = [x[p + 4] * root for p in range(4)]
    plus = [x[p] + s[p] for p in range(4)]
    minus = [x[p] - s[p] for p in range(4)]
    out = [None] * 8
    for m in range(4):
        v = []
        for p in range(4):
            re = plus[p] if m in (0, 3) else minus[p]
            im = s[p]
            sign = -1.0 if m in (0, 1) else 1.0
            if p == 0:
                v.append((re, im if sign > 0 else -im))
            else:
                a = math.pi * (2 * m + 1) * p / 16
                wr, wi = math.cos(a), -math.sin(a)
                v.append((re * wr - im * (sign * wi), re * wi + im * (sign * wr)))
        e = (v[0][0] + v[2][0], v[0][1] + v[2][1])
        d = (v[0][0] - v[2][0], v[0][1] - v[2][1])
        f = (v[1][0] + v[3][0], v[1][1] + v[3][1])
        h = (v[1][0] - v[3][0], v[1][1] - v[3][1])
        out[m] = (e[0] + f[0], e[1] + f[1])
        out[m + 4] = (d[0] + h[1], d[1] - h[0])
    return out


def eight(z):
    add = lambda a, b: (a[0] + b[0], a[1] + b[1])
    sub = lambda a, b: (a[0] - b[0], a[1] - b[1])
    turn = lambda a: (a[1], -a[0])

    def four(a, b, c, d):
        e, f, g, h = add(a, c), sub(a, c), add(b, d), turn(sub(b, d))
        return add(e, g), add(f, h), sub(e, g), sub(f, h)

    even, odd = four(z[0], z[2], z[4], z[6]), four(z[1], z[3], z[5], z[7])
    root = math.sqrt(0.5)
    o1 = ((odd[1][0] + odd[1][1]) * root, (odd[1][1] - odd[1][0]) * root)
    o3 = ((odd[3][1] - odd[3][0]) * root, -(odd[3][0] + odd[3][1]) * root)
    turned = (odd[0], o1, turn(odd[2]), o3)
    return [add(even[k], turned[k]) for k in range(4)] + [sub(even[k], turned[k]) for k in range(4)]


def outer_first(load, mid_ref):
    for q2 in range(4):
        for half in range(2):
            out = first_step([load(4 * p + q2, half) for p in range(8)])
            for m in range(8):
                mid_ref[m, 2 * q2 + half, 0] = out[m][0]
                mid_ref[m, 2 * q2 + half, 1] = out[m][1]


def outer_second(twist_ref, mid_ref, y_ref, start=0, stop=8):
    for m in range(start, stop):
        z = []
        for q in range(8):
            re, im = mid_ref[m, q, 0], mid_ref[m, q, 1]
            a = math.pi * (2 * m + 1) * q / 128
            z.append((re, im) if q == 0 else cmul(re, im, math.cos(a), -math.sin(a)))
        done = []
        for n, (re, im) in enumerate(eight(z)):
            row = 8 * m + n
            done.append(cmul(re, im, twist_ref[row : row + 1, 0:128], -twist_ref[row : row + 1, 128:256]))
        for n in range(0, 8, 2):
            for part in range(2):
                pair = split(jnp.concatenate([done[n][part], done[n + 1][part]], axis=0))
                for k in range(2):
                    y_ref[k, (8 * m + n) * 8 : (8 * m + n) * 8 + 16, part * 128 : part * 128 + 128] = pair[k]


def inner(y_ref, at, count, table):
    return dot3((y_ref[0, at : at + count], y_ref[1, at : at + count]), table)


def channel_sums(rows):
    lane = lax.broadcasted_iota(jnp.int32, (8, 128), 0)
    low = lane < 4
    out = []
    for k in range(4):
        a, b = rows[k], rows[k + 4]
        out.append(jnp.where(low, a, b) + pltpu.roll(jnp.where(low, b, a), 4, 0))
    for width in (2, 1):
        keep = lane % (2 * width) < width
        out = [
            jnp.where(keep, a + pltpu.roll(a, 8 - width, 0), b + pltpu.roll(b, width, 0))
            for a, b in zip(out[:width], out[width:])
        ]
    return out[0]


def multiply(grads, spec_ref, at, acc_ref):
    for m in range(grads.shape[0] // 64):
        re, im = [], []
        for n in range(8):
            row = m * 64 + n * 8
            gr, gi = grads[row : row + 8, 0:128], grads[row : row + 8, 128:256]
            ur, ui = spec_ref[at + row : at + row + 8, 0:128], spec_ref[at + row : at + row + 8, 128:256]
            re.append(gr * ur + gi * ui)
            im.append(gi * ur - gr * ui)
        to = at // 8 + m * 8
        acc_ref[to : to + 8, 0:128] += channel_sums(re)
        acc_ref[to : to + 8, 128:256] += channel_sums(im)


def fused_kernel(tiles_hbm, lags_hbm, u_ref, g_ref, *refs):
    tables_hbm, refs = refs[:6], refs[6:]
    out, refs = refs[0], refs[1:]
    tables_vmem, refs = refs[:6], refs[6:]
    fh, fl, ih, il, twist, ends = tables_vmem
    (tiles, lags, slots, xin, turned, mid, land, stage, stage_b, mid_ref, mid_b, y_a, y_b, spec_ref, acc_ref, ends_f, ends_b, blocks, land_o,
     owned, square, tally,
     insem, ordsem, tabsem, s_a, r_a, s_b, r_b, l_a, l_b, s_ao, r_ao, s_q, r_q, l_o, line_sem, far_sem) = refs
    z, x, c = place()
    ch = lax.axis_index("ch")

    def at(dz, dx, dc, dy):
        return (((z + dz) % SIDE) * 8 + ((x + dx) % SIDE) * 2 + (c + dc) % 2, (ch + dy) % SIDE)

    def shift(kind, d, k, e):
        return at(e, d, k, 0) if kind == 0 else at(d, e, k, 0)

    others = [(dz, dx, k, dy) for dz in HOPS for dx in HOPS for k in (1, 0) for dy in HOPS]
    others.remove((0, 0, 0, 0))
    others.sort(key=lambda move: -sum(min(d, SIDE - d) for d in (move[0], move[1], move[3])))
    column = [(0, 0, 0, d) for d in HOPS[:3]]
    line = [(d, 0, 0, 0) for d in HOPS[:3]]
    plane = [(dz, dx, k) for dz in HOPS for dx in HOPS for k in (1, 0) if (dz, dx, k) != (0, 0, 0)]
    plane.sort(key=lambda move: -min(move[0], SIDE - move[0]) - min(move[1], SIDE - move[1]))
    peers = {(0, d, k, 0) for d, k in MOVES} | {(d, 0, k, 0) for d, k in MOVES} | set(column)
    barrier = pltpu.get_barrier_semaphore()
    for peer in sorted(peers):
        pl.semaphore_signal(barrier, inc=1, device_id=at(*peer), device_id_type=MESH)

    mine = ((x, z), (z, x))
    incoming = []
    for arr, ref in enumerate((u_ref, g_ref)):
        for step in HOPS:
            for kind in range(2):
                a = (mine[kind][0] + step) % SIDE
                n = len(incoming)
                copy = pltpu.make_async_copy(
                    ref.at[:, pl.ds(pl.multiple_of(kind * 512 + a * 128, 128), 128)], xin.at[n], insem.at[n]
                )
                copy.start()
                incoming.append((copy, step, kind, a, arr))
    order_copies = [
        pltpu.make_async_copy(tiles_hbm, tiles, ordsem.at[0]),
        pltpu.make_async_copy(lags_hbm, lags, ordsem.at[1]),
    ]
    for copy in order_copies:
        copy.start()
    table_copies = [pltpu.make_async_copy(h, v, tabsem.at[n]) for n, (h, v) in enumerate(zip(tables_hbm, tables_vmem))]
    for copy in table_copies:
        copy.start()

    def send_a(kind, kh, arr, move):
        d, k = MOVES[move]
        a = mine[kind][0]
        return pltpu.make_async_remote_copy(
            src_ref=turned.at[kind, (a + d) % SIDE, (c + k) % 2, :, kh, arr],
            dst_ref=mid.at[kind, kh, arr, :, a * 2 + c],
            send_sem=s_a.at[kind, kh, arr, move],
            recv_sem=r_a.at[kind, kh, arr, move],
            device_id=shift(kind, d, k, 0),
            device_id_type=MESH,
        )

    def own_a(kind, kh, arr):
        a = mine[kind][0]
        return pltpu.make_async_copy(
            turned.at[kind, a, c, :, kh, arr], mid.at[kind, kh, arr, :, a * 2 + c], l_a.at[kind, kh, arr]
        )

    def send_b(kind, kh, arr, hop):
        b = mine[kind][1]
        return pltpu.make_async_remote_copy(
            src_ref=mid.at[kind, kh, arr, (b + HOPS[hop]) % SIDE],
            dst_ref=land.at[kind, kh, arr, pl.ds(b * 8, 8)],
            send_sem=s_b.at[kind, kh, arr, hop],
            recv_sem=r_b.at[kind, kh, arr, hop],
            device_id=shift(kind, 0, 0, HOPS[hop]),
            device_id_type=MESH,
        )

    def own_b(kind, kh, arr):
        b = mine[kind][1]
        return pltpu.make_async_copy(
            mid.at[kind, kh, arr, b], land.at[kind, kh, arr, pl.ds(b * 8, 8)], l_b.at[kind, kh, arr]
        )

    def turn(n):
        copy, step, kind, a, arr = incoming[n]
        copy.wait()
        turned[kind, a, :, :, :, arr] = xin[n].T.reshape(2, 4, 2, 8, 256)

    def begin(n):
        _, step, kind, a, arr = incoming[n]
        for move, (d, k) in enumerate(MOVES):
            if d == step:
                send_a(kind, 0, arr, move).start()

    early = 4
    for n in range(early):
        turn(n)
    pl.semaphore_wait(barrier, len(peers))
    for n in range(early):
        begin(n)
    for n in range(early, len(incoming)):
        turn(n)
        begin(n)
    for arr in range(2):
        for move in range(len(MOVES)):
            for kind in range(2):
                send_a(kind, 1, arr, move).start()
    for kh in range(2):
        for arr in range(2):
            for kind in range(2):
                own_a(kind, kh, arr).start()
    for peer in line:
        pl.semaphore_signal(line_sem, inc=1, device_id=at(*peer), device_id_type=MESH)

    for copy in order_copies:
        copy.wait()

    def find(tile, carry):
        first, second = jnp.int32(0), jnp.int32(0)
        for s in range(32):
            zz, xx, cc = s // 8, (s // 2) % 4, s % 2
            hit = tiles[s] == tile
            first = jnp.where(hit, s, first)
            second = jnp.where(hit, xx * 8 + zz * 2 + cc, second)
        slots[0, tile] = first
        slots[1, tile] = second
        return carry

    lax.fori_loop(0, 32, find, 0)

    def forward(kh, arr):
        for kind in range(2):
            own_a(kind, kh, arr).wait()
            for move in range(len(MOVES)):
                send_a(kind, kh, arr, move).wait_recv()
            for hop in range(3):
                send_b(kind, kh, arr, hop).start()
            own_b(kind, kh, arr).start()

    pl.semaphore_wait(line_sem, len(line))
    for peer in column:
        pl.semaphore_signal(far_sem, inc=1, device_id=at(*peer), device_id_type=MESH)
    forward(0, 0)
    for copy in table_copies:
        copy.wait()
    acc_ref[...] = jnp.zeros_like(acc_ref)
    for t in range(32):
        xc, zz = t // 4, t % 4
        block = lags[zz * 8 + xc]
        for half in range(2):
            ends_f[half * 32 + t : half * 32 + t + 1, :] = ends[pl.ds(half * 32 + block, 1), :]
    high, low = split(ends_f[...])
    ends_b[0] = high
    ends_b[1] = low
    forward(0, 1)
    forward(1, 0)
    forward(1, 1)
    inner_table = (fh[...], fl[...])

    def take(kind, kh, arr, held=stage):
        own_b(kind, kh, arr).wait()
        for hop in range(3):
            send_b(kind, kh, arr, hop).wait_recv()
        held[...] = land[kind, kh, arr]
        return lambda tile, half: held[slots[kind, tile], :, half * 128 : half * 128 + 128]

    def spectra(kind, y_ref):
        spec_ref[kind] = inner(y_ref, 0, ROWS * 8, inner_table)

    def products(kind, y_ref, part):
        grads = inner(y_ref, part * PART, PART, inner_table)
        multiply(grads, spec_ref.at[kind], part * PART, acc_ref.at[kind])

    def chunk(kh, carry):
        outer_first(take(0, kh, 0), mid_ref)
        outer_second(twist, mid_ref, y_a)
        load = take(1, kh, 0)
        spectra(0, y_a)
        outer_first(load, mid_ref)
        outer_second(twist, mid_ref, y_b)
        spectra(1, y_b)
        load = take(0, kh, 1)
        later = take(1, kh, 1, stage_b)
        outer_first(load, mid_ref)
        for part in range(PARTS):
            outer_second(twist, mid_ref, y_a, part * 8 // PARTS, (part + 1) * 8 // PARTS)
            products(0, y_a, part)
        outer_first(later, mid_b)
        for part in range(PARTS):
            outer_second(twist, mid_b, y_b, part * 8 // PARTS, (part + 1) * 8 // PARTS)
            products(1, y_b, part)
        return carry

    lax.fori_loop(0, 2, chunk, 0)

    back = (ih[...], il[...])
    sides = []
    for kind in range(2):
        v = dot3(split(acc_ref[kind]), back)
        re, im = cmul(v[:, 0:128], v[:, 128:256], twist[:, 0:128], twist[:, 128:256])
        sides.append(jnp.concatenate([re, im], axis=0))
    high, low = split(jnp.concatenate(sides, axis=1))
    dot = functools.partial(jnp.dot, preferred_element_type=F32)
    values = dot(ends_b[0], high) + (dot(ends_b[0], low) + dot(ends_b[1], high))

    def send_q(k):
        return pltpu.make_async_remote_copy(
            src_ref=square, dst_ref=tally.at[k], send_sem=s_q, recv_sem=r_q, device_id=at(*others[k]), device_id_type=MESH
        )

    every_q = pltpu.make_async_remote_copy(
        src_ref=tally, dst_ref=tally, send_sem=s_q, recv_sem=r_q, device_id=at(*others[0]), device_id_type=MESH
    )

    def send_ao(move):
        dz, dx, k = plane[move]
        to = (((x + dx) % SIDE) * 2 + (c + k) % 2) * 4 + (z + dz) % SIDE
        return pltpu.make_async_remote_copy(
            src_ref=blocks.at[pl.ds(to * 8, 8)],
            dst_ref=land_o.at[z * 8 + x * 2 + c],
            send_sem=s_ao.at[move],
            recv_sem=r_ao.at[move],
            device_id=at(dz, dx, k, 0),
            device_id_type=MESH,
        )

    both = values[:, 0:128] * values[:, 0:128] + values[:, 128:256] * values[:, 128:256]
    own_square = jnp.sum(both, axis=0, keepdims=True)
    square[...] = own_square
    pl.semaphore_wait(far_sem, len(column))
    for k in range(len(others)):
        send_q(k).start()
    for kind in range(2):
        for half in range(2):
            blocks[pl.ds(2 * kind + half, 32, stride=8), :] = values[half * 32 : half * 32 + 32, kind * 128 : kind * 128 + 128]
    for move in range(len(plane)):
        send_ao(move).start()
    own_ao = pltpu.make_async_copy(blocks.at[pl.ds(((x * 2 + c) * 4 + z) * 8, 8)], land_o.at[z * 8 + x * 2 + c], l_o)
    own_ao.start()
    for kh in range(2):
        for arr in range(2):
            for kind in range(2):
                for move in range(len(MOVES)):
                    send_a(kind, kh, arr, move).wait_send()
                for hop in range(3):
                    send_b(kind, kh, arr, hop).wait_send()
    own_ao.wait()
    for move in range(len(plane)):
        send_ao(move).wait()
    rows = land_o.reshape(256, 128)
    for zz in range(4):
        for half in range(2):
            owned[pl.ds(half * 64 + zz, 8, stride=4), :] = rows[pl.ds(zz * 64 + half, 8, stride=8), :]
            for cc in range(2):
                to = half * 64 + 32 + 8 * zz + 4 * cc
                owned[to : to + 4, :] = rows[pl.ds(zz * 64 + cc * 8 + 2 + half, 4, stride=16), :]
    every_q.wait_send()
    every_q.wait_recv()
    total = jnp.sum(own_square + jnp.sum(tally[...], axis=0), axis=1, keepdims=True)
    total_entries = C // GROUP * POS // 2
    factor = target_ratio * math.sqrt(total_entries) / jnp.sqrt(total + epsilon)
    out[:, 0:128] = owned[0:64] * factor
    out[:, 128:256] = owned[64:128] * factor


def shards(inputs, out_grads, tile_order, lag_order):
    vmem = pl.BlockSpec(memory_space=pltpu.VMEM)
    hbm = pl.BlockSpec(memory_space=pl.ANY)
    dma = pltpu.SemaphoreType.DMA
    consts = [jnp.asarray(t) for t in tables()]
    return pl.pallas_call(
        fused_kernel,
        out_shape=pltpu.VMEM((64, 256), F32),
        in_specs=[hbm] * 10,
        out_specs=vmem,
        scratch_shapes=[pltpu.VMEM(t.shape, t.dtype) for t in consts]
        + [
            pltpu.SMEM((32,), jnp.int32),
            pltpu.SMEM((32,), jnp.int32),
            pltpu.SMEM((2, 32), jnp.int32),
            pltpu.VMEM((16, 256, 128), F32),
            pltpu.VMEM((2, 4, 2, 4, 2, 2, 8, 256), F32),
            pltpu.VMEM((2, 2, 2, 4, 8, 8, 256), F32),
            pltpu.VMEM((2, 2, 2, 32, 8, 256), F32),
            pltpu.VMEM((32, 8, 256), F32),
            pltpu.VMEM((32, 8, 256), F32),
            pltpu.VMEM((8, 8, 2, 8, 128), F32),
            pltpu.VMEM((8, 8, 2, 8, 128), F32),
            pltpu.VMEM((2, ROWS * 8, 256), BF16),
            pltpu.VMEM((2, ROWS * 8, 256), BF16),
            pltpu.VMEM((2, ROWS * 8, 256), F32),
            pltpu.VMEM((2, ROWS, 256), F32),
            pltpu.VMEM((ROWS, 128), F32),
            pltpu.VMEM((2, ROWS, 128), BF16),
            pltpu.VMEM((256, 128), F32),
            pltpu.VMEM((32, 8, 128), F32),
            pltpu.VMEM((128, 128), F32),
            pltpu.VMEM((1, 128), F32),
            pltpu.VMEM((127, 1, 128), F32),
            dma((16,)), dma((2,)), dma((6,)), dma((2, 2, 2, 7)), dma((2, 2, 2, 7)), dma((2, 2, 2, 3)), dma((2, 2, 2, 3)),
            dma((2, 2, 2)), dma((2, 2, 2)), dma((31,)), dma((31,)), dma, dma, dma, pltpu.SemaphoreType.REGULAR, pltpu.SemaphoreType.REGULAR,
        ],
        compiler_params=pltpu.CompilerParams(collective_id=0, has_side_effects=True),
    )(tile_order, lag_order, inputs, out_grads, *consts)


def solution(mesh):
    return jax.shard_map(
        shards,
        mesh=mesh,
        in_specs=(P("seq", "ch"), P("seq", "ch"), P(), P()),
        out_specs=P("ch", "seq"),
        check_vma=False,
    )
```
